32 devices in a mesh: beam: 4 (over z), pulse: 4 (over x, core), range: 2 (over y).
Axes of the slice: x: 2, y: 2, z: 4, core: 2. Of those that a mesh axis runs over, the one named last changes fastest.
Arguments:
- signal: bfloat16 [8, 32, 2, 1024], P('beam', 'pulse', None, 'range'), may hold values from -40 to 40, as said below
- replica: bfloat16 [2, 2048], P(None, ('beam', 'pulse')), may hold values from -0.09375 to 0.09375
- guard_cells: int32 [8], P('beam'), may hold values from 1 to 8, as said below
- train_cells: int32 [8], P('beam'), may hold values from 64 to 96, as said below
- scale_index: int32 [8], P('beam'), may hold values from 0 to 15
- offsets: int32 [8], P('beam'), may hold values from 0 to 127, as said below
Outputs:
- compressed: bfloat16 [8, 32, 2, 1024], P('beam', 'pulse', None, 'range')
- test_ratio: float32 [8, 32, 1024], P('beam', 'pulse', 'range')
The draws below stay inside these ranges and needn't reach their ends.
Inputs may be any that keep to these rules, and one draw needn't show every extreme that they name: `signal`: values stay within the range, with cell-to-cell varying levels. `guard_cells`: some beam has exactly 8 guard cells. `train_cells`: the beam with 8 guard cells has 96 training cells. `offsets`: some beam has the offset 128 - 1.
All inputs are finite; a program needn't handle non-finite values.
Results may differ from the reference program's by a relative error of at most 0.001.
Values may be sent and summed in bfloat16 or wider, within the bound.
A program may use at most 64 MiB of HBM per device.

```python
import jax
import jax.numpy as jnp
from jax import lax

TAPS = 2048
OFF_MAX = 128
GUARD_MAX = 8
TRAIN_MIN = 64
TRAIN_MAX = 96
BEAMS = 8
PULSES = 32
GATES = 1024


def chosen_beam(key):
    return jax.random.randint(jax.random.fold_in(key, 101), (), 0, BEAMS)


def draw_signal(key, part):
    shape = (BEAMS, PULSES, 2, GATES)
    base = jnp.clip(jax.random.normal(jax.random.fold_in(key, 11), shape, jnp.float32), -6.0, 6.0)
    levels = jnp.exp(jax.random.uniform(jax.random.fold_in(key, 12), (BEAMS, 1, 1, GATES), jnp.float32, -1.15, 1.15))
    values = base * levels
    return values.astype(jnp.bfloat16)


def draw_guard_cells(key, part):
    values = jax.random.randint(jax.random.fold_in(key, 1), (BEAMS,), 1, GUARD_MAX + 1)
    return values.at[chosen_beam(key)].set(GUARD_MAX).astype(jnp.int32)


def draw_train_cells(key, part):
    values = jax.random.randint(jax.random.fold_in(key, 2), (BEAMS,), TRAIN_MIN, TRAIN_MAX + 1)
    return values.at[chosen_beam(key)].set(TRAIN_MAX).astype(jnp.int32)


def draw_offsets(key, part):
    values = jax.random.randint(jax.random.fold_in(key, 3), (BEAMS,), 0, OFF_MAX)
    return values.at[chosen_beam(key)].set(OFF_MAX - 1).astype(jnp.int32)


def plant(entries, stream_key, low, top_value):
    longest = entries.shape.index(max(entries.shape))
    spots = []
    for shift in (0, 1):
        where = [jax.random.randint(jax.random.fold_in(stream_key, axis), (), 0, length) for axis, length in enumerate(entries.shape)]
        where[longest] = (where[longest] + shift) % entries.shape[longest]
        spots.append(tuple(where))
    return entries.at[spots[0]].set(low).at[spots[1]].set(top_value)


def shard_levels(key, shape, pieces, smallest, largest):
    loudness = 1.0
    for axis_at, shards_of in pieces:
        steps = jax.random.uniform(jax.random.fold_in(jax.random.fold_in(key, 6), axis_at), (shards_of,), jnp.float32, smallest / len(pieces), largest / len(pieces))
        loudness = loudness * jnp.repeat(jnp.exp(steps), shape[axis_at] // shards_of).reshape((-1,) + (1,) * (len(shape) - 1 - axis_at))
    return loudness


def scatter_about(key, extent, width, reach, shards=(), kind=jnp.bfloat16):
    entries = width * jax.random.normal(key, extent, jnp.float32)
    if shards:
        entries = entries * shard_levels(key, extent, shards, -0.22, 0.18)
    return jnp.clip(entries, -reach, reach).astype(kind)


def setup_inputs(seed: int = 0) -> dict:
    seeds = jax.random.split(jax.random.key(seed), 7)
    signal = draw_signal(jax.random.fold_in(seeds[6], 71), 0)
    replica = scatter_about(seeds[1], (2, TAPS), (2 * TAPS) ** -0.5, 0.09375, ((1, 16),))
    guard_cells = draw_guard_cells(jax.random.fold_in(seeds[6], 71), 0)
    train_cells = draw_train_cells(jax.random.fold_in(seeds[6], 71), 0)
    scale_index = plant(jax.random.randint(seeds[4], (BEAMS,), 0, 16), jax.random.fold_in(seeds[4], 1), 0, 15).astype(jnp.int32)
    offsets = draw_offsets(jax.random.fold_in(seeds[6], 71), 0)
    return {"signal": signal, "replica": replica, "guard_cells": guard_cells, "train_cells": train_cells, "scale_index": scale_index, "offsets": offsets}


EPSILON = 1e-6


def strip_ratio(power, guard, train, level, gates):
    margin = GUARD_MAX + TRAIN_MAX
    padded = jnp.pad(power, ((0, 0), (margin, margin)))
    prefix = jnp.concatenate([jnp.zeros((power.shape[0], 1), jnp.float32), jnp.cumsum(padded, axis=1)], axis=1)
    position = jnp.arange(gates, dtype=jnp.int32)
    centre = position + margin
    lag = jnp.take(prefix, centre - guard, axis=1) - jnp.take(prefix, centre - guard - train, axis=1)
    lead = jnp.take(prefix, centre + guard + train + 1, axis=1) - jnp.take(prefix, centre + guard + 1, axis=1)
    count = jnp.clip(position - guard, 0, train) + jnp.clip(gates - 1 - position - guard, 0, train)
    noise = (lag + lead) / count.astype(jnp.float32)[None, :]
    factor = jnp.exp2(level.astype(jnp.float32) / 8.0)
    return power / (factor * (noise + EPSILON))


def reference(signal, replica, guard_cells, train_cells, scale_index, offsets):
    gates = signal.shape[3]
    length = 1
    while length < gates + TAPS + OFF_MAX:
        length = length * 2
    taps_values = replica.astype(jnp.float32)
    kernel = jnp.conj(jnp.fft.fft(taps_values[0] + 1j * taps_values[1], length))

    def one(items):
        block, start, guard, train, level = items
        values = block.astype(jnp.float32)
        spectrum = jnp.fft.fft(values[:, 0] + 1j * values[:, 1], length, axis=-1)
        corr = jnp.fft.ifft(spectrum * kernel[None, :], axis=-1)
        window = lax.dynamic_slice_in_dim(corr, start.astype(jnp.int32), gates, 1)
        result = jnp.stack([jnp.real(window), jnp.imag(window)], axis=1).astype(jnp.float32).astype(jnp.bfloat16)
        real_part = result[:, 0].astype(jnp.float32)
        imag_part = result[:, 1].astype(jnp.float32)
        power = real_part * real_part + imag_part * imag_part
        return result, strip_ratio(power, guard, train, level, gates)

    compressed, test_ratio = lax.map(one, (signal, offsets, guard_cells, train_cells, scale_index))
    return compressed, test_ratio
```

```python
import functools

import jax
import jax.numpy as jnp
from jax import lax
from jax.experimental import pallas as pl
from jax.experimental.pallas import tpu as pltpu
from jax.sharding import PartitionSpec as P

TILE = 128
OFF_MAX = 128
EPSILON = 1e-06
MESH = pl.DeviceIdType.MESH


def plan(signal, replica, sizes):
    nb, npulse, nr = sizes
    pieces = nb * npulse
    piece = replica[1]
    gates = signal[3]
    total = gates * nr
    taps = min(piece * pieces, total)
    senders = -(-taps // piece)
    tiles = gates // TILE + 2
    panels = min(-(-piece * pieces // TILE) + 1, total // TILE)
    chunks = min(tiles + panels - 1, total // TILE + 1)
    beyond = (chunks - 1) * TILE - gates + OFF_MAX
    reach = min(-(-beyond // gates), nr - 1)
    keeps = [min(gates, beyond - s * gates) for s in range(reach)]
    return pieces, piece, gates, total, senders, tiles, panels, chunks, keeps


def kernel(
    sizes, dims, offsets, guards, trains, scales, sig, rep, comp, ratio, *scratch
):
    pieces, piece, gates, total, senders, tiles, panels, chunks, keeps = dims
    nb, npulse, nr = sizes
    beams, pulses = sig.shape[0], sig.shape[1]
    rows = beams * pulses
    hbuf, left, xf, xa, yf, hsend, hrecv, xsend, xrecv = scratch[:9]
    right = scratch[9:]
    bi, pi, ri = lax.axis_index("beam"), lax.axis_index("pulse"), lax.axis_index("range")
    me = bi * npulse + pi
    reach = len(keeps)

    def where_is(index):
        return {"beam": index // npulse, "pulse": index % npulse}

    barrier = pltpu.get_barrier_semaphore()
    for s in range(senders):

        @pl.when(me != s)
        def _():
            pl.semaphore_signal(
                barrier, inc=1, device_id=where_is(s), device_id_type=MESH
            )

    for s in range(1, reach + 1):

        @pl.when(ri + s < nr)
        def _():
            pl.semaphore_signal(
                barrier, inc=1, device_id={"range": ri + s}, device_id_type=MESH
            )

    @pl.when(ri >= 1)
    def _():
        pl.semaphore_signal(
            barrier, inc=1, device_id={"range": ri - 1}, device_id_type=MESH
        )

    def head_copy(s):
        return pltpu.make_async_remote_copy(
            src_ref=sig.at[:, :, :, pl.ds(0, keeps[s - 1])],
            dst_ref=right[s - 1],
            send_sem=xsend.at[s],
            recv_sem=xrecv.at[s],
            device_id={"range": ri - s},
            device_id_type=MESH,
        )

    def tail_copy():
        return pltpu.make_async_remote_copy(
            src_ref=sig.at[:, :, :, pl.ds(gates - TILE, TILE)],
            dst_ref=left,
            send_sem=xsend.at[0],
            recv_sem=xrecv.at[0],
            device_id={"range": ri + 1},
            device_id_type=MESH,
        )

    def tap_copy(slot, step, target):
        return pltpu.make_async_remote_copy(
            src_ref=rep,
            dst_ref=hbuf.at[slot],
            send_sem=hsend.at[step],
            recv_sem=hrecv.at[slot],
            device_id=where_is(target),
            device_id_type=MESH,
        )

    expect = jnp.minimum(ri, reach) + jnp.where(ri + 1 < nr, 1, 0)
    pl.semaphore_wait(barrier, expect + jnp.where(me < senders, pieces - 1, 0))

    @pl.when(me < senders)
    def _():
        for step in range(pieces - 1, 0, -1):
            tap_copy(me, step, lax.rem(me + step, pieces)).start()

    for s in range(1, reach + 1):

        @pl.when(ri - s >= 0)
        def _():
            head_copy(s).start()

    @pl.when(ri + 1 < nr)
    def _():
        tail_copy().start()

    @pl.when(me < senders)
    def _():
        hbuf[me] = rep[...]

    def place(source, start, width):
        for b in range(beams):
            for p in range(pulses):
                at = 2 * (b * pulses + p)
                pair = source[b, p].astype(jnp.float32)
                for c in range(width // TILE):
                    xf[start // TILE + c, at : at + 2, :] = pair[:, c * TILE : (c + 1) * TILE]

    def clear(start, stop):
        for c in range(start // TILE, stop // TILE):
            xf[c] = jnp.zeros((2 * rows, TILE), jnp.float32)

    place(sig, TILE, gates)
    tail = TILE + gates + sum(keeps)
    width = yf.shape[1]
    clear(tail, width)

    across = tiles - 2
    lane = lax.broadcasted_iota(jnp.int32, (TILE, 3 * TILE), 1)
    row = lax.broadcasted_iota(jnp.int32, (TILE, 3 * TILE), 0)
    apart = jnp.abs(lane - TILE - row)
    position = ri * gates + lax.broadcasted_iota(jnp.int32, (pulses, gates), 1)
    weights, counts, factors = [], [], []
    for b in range(beams):
        guard, train = guards[b], trains[b]
        inside = (apart > guard) & (apart <= guard + train)
        weights.append(jnp.where(inside, 1.0, 0.0).astype(jnp.bfloat16))
        count = jnp.clip(position - guard, 0, train) + jnp.clip(
            total - 1 - position - guard, 0, train
        )
        counts.append(count.astype(jnp.float32))
        level = jnp.full((pulses, TILE), scales[b], jnp.int32).astype(jnp.float32)
        factors.append(jnp.exp2(level / 8.0))

    @pl.when(ri >= 1)
    def _():
        tail_copy().wait_recv()
        place(left, 0, TILE)

    @pl.when(ri == 0)
    def _():
        clear(0, TILE)

    at = TILE + gates
    for s in range(1, reach + 1):
        start, keep = at, keeps[s - 1]

        @pl.when(ri + s < nr)
        def _():
            head_copy(s).wait_recv()
            place(right[s - 1], start, keep)

        @pl.when(ri + s >= nr)
        def _():
            clear(start, start + keep)

        at += keep

    for b in range(beams):
        low = 2 * b * pulses
        real, imag = [
            pltpu.roll(
                jnp.concatenate(
                    [
                        xf[c, pl.ds(low + part, pulses, stride=2), :]
                        for c in range(width // TILE)
                    ],
                    axis=1,
                ),
                width - offsets[b],
                1,
            )
            for part in range(2)
        ]
        yf[b * pulses : (b + 1) * pulses, :] = real
        yf[rows + b * pulses : rows + (b + 1) * pulses, :] = imag
    for c in range(chunks):
        real = yf[:rows, c * TILE : (c + 1) * TILE]
        imag = yf[rows:, c * TILE : (c + 1) * TILE]
        first = jnp.concatenate([real, imag], axis=1)
        second = jnp.concatenate([imag, -real], axis=1)
        xa[c] = jnp.concatenate([first, second], axis=0).astype(jnp.bfloat16)

    for s in range(senders):

        @pl.when(me != s)
        def _():
            tap_copy(s, 0, me).wait_recv()

    per = TILE // piece if piece < TILE else 1
    spread = max(piece // TILE, 1)

    def taps_of(c):
        if piece >= TILE:
            return hbuf[c // spread].astype(jnp.float32)[
                :, (c % spread) * TILE : (c % spread + 1) * TILE
            ]
        parts = [hbuf[c * per + i].astype(jnp.float32) for i in range(per)]
        return jnp.concatenate(parts, axis=1)

    held = min(panels, (senders * piece) // TILE)
    lane = lax.broadcasted_iota(jnp.int32, (TILE, TILE), 1)
    row = lax.broadcasted_iota(jnp.int32, (TILE, TILE), 0)
    ahead = lane >= row

    def skewed(values):
        flat = jnp.broadcast_to(values, (TILE, TILE))
        return pltpu.roll(flat, 0, 1, stride=1, stride_axis=0)

    zero = jnp.zeros((TILE, TILE), jnp.float32)
    before = (zero, zero)
    sums = [None] * tiles
    for c in range(panels):
        if c < held:
            taps = taps_of(c)
            now = (skewed(taps[0:1]), skewed(taps[1:2]))
        else:
            now = (zero, zero)
        panel = jnp.concatenate(
            [jnp.where(ahead, n, b) for n, b in zip(now, before)], axis=1
        ).astype(jnp.bfloat16)
        before = now
        n = min(tiles, chunks - c)
        left_side = xa[c : c + n].reshape(n * 2 * rows, 2 * TILE)
        product = lax.dot_general(
            left_side, panel, (((1,), (1,)), ((), ())), preferred_element_type=jnp.float32
        )
        for i in range(n):
            part = product[i * 2 * rows : (i + 1) * 2 * rows]
            sums[i] = part if sums[i] is None else sums[i] + part

    powers = []
    for i in range(tiles):
        rounded = sums[i].astype(jnp.bfloat16).astype(jnp.float32)
        real, imag = rounded[:rows], rounded[rows:]
        power = real * real + imag * imag
        if i == 0:
            power = jnp.where(ri >= 1, power, 0.0)
        powers.append(power)
        if 1 <= i <= across:
            xf[i - 1, pl.ds(0, rows, stride=2), :] = real
            xf[i - 1, pl.ds(1, rows, stride=2), :] = imag
    for b in range(beams):
        for p in range(pulses):
            at = 2 * (b * pulses + p)
            for i in range(across):
                comp[b, p, :, i * TILE : (i + 1) * TILE] = xf[i, at : at + 2, :].astype(
                    jnp.bfloat16
                )

    split = []
    for power in powers:
        high = power.astype(jnp.bfloat16)
        rest = power - high.astype(jnp.float32)
        middle = rest.astype(jnp.bfloat16)
        low = (rest - middle.astype(jnp.float32)).astype(jnp.bfloat16)
        split.append([v.astype(jnp.float32) for v in (high, middle, low)])
    for b in range(beams):
        mine = slice(b * pulses, (b + 1) * pulses)
        side = jnp.concatenate(
            [
                jnp.concatenate([split[i + d][k][mine] for d in range(3)], axis=1)
                for i in range(across)
                for k in range(3)
            ],
            axis=0,
        ).astype(jnp.bfloat16)
        window = lax.dot_general(
            side, weights[b], (((1,), (1,)), ((), ())), preferred_element_type=jnp.float32
        )
        for i in range(across):
            base = 3 * i * pulses
            noise = (
                window[base : base + pulses]
                + window[base + pulses : base + 2 * pulses]
                + window[base + 2 * pulses : base + 3 * pulses]
            ) / counts[b][:, i * TILE : (i + 1) * TILE]
            ratio[b, :, i * TILE : (i + 1) * TILE] = powers[i + 1][mine] / (
                factors[b] * (noise + EPSILON)
            )

    @pl.when(me < senders)
    def _():
        for step in range(1, pieces):
            tap_copy(me, step, me).wait_send()

    for s in range(1, reach + 1):

        @pl.when(ri - s >= 0)
        def _():
            head_copy(s).wait_send()

    @pl.when(ri + 1 < nr)
    def _():
        tail_copy().wait_send()


def body(sizes, signal, replica, guard_cells, train_cells, scale_index, offsets):
    dims = plan(signal.shape, replica.shape, sizes)
    pieces, piece, gates, total, senders, tiles, panels, chunks, keeps = dims
    beams, pulses = signal.shape[0], signal.shape[1]
    rows = beams * pulses
    width = max(chunks * TILE + OFF_MAX, TILE + gates + sum(keeps))
    smem = pl.BlockSpec(memory_space=pltpu.SMEM)
    vmem = pl.BlockSpec(memory_space=pltpu.VMEM)
    return pl.pallas_call(
        functools.partial(kernel, sizes, dims),
        out_shape=(
            jax.ShapeDtypeStruct(signal.shape, jnp.bfloat16),
            jax.ShapeDtypeStruct((beams, pulses, gates), jnp.float32),
        ),
        in_specs=[smem] * 4 + [vmem] * 2,
        out_specs=(vmem, vmem),
        scratch_shapes=[
            pltpu.VMEM((senders, 2, piece), jnp.bfloat16),
            pltpu.VMEM((beams, pulses, 2, TILE), jnp.bfloat16),
            pltpu.VMEM((width // TILE, 2 * rows, TILE), jnp.float32),
            pltpu.VMEM((chunks, 2 * rows, 2 * TILE), jnp.bfloat16),
            pltpu.VMEM((2 * rows, width), jnp.float32),
            pltpu.SemaphoreType.DMA((pieces,)),
            pltpu.SemaphoreType.DMA((senders,)),
            pltpu.SemaphoreType.DMA((len(keeps) + 1,)),
            pltpu.SemaphoreType.DMA((len(keeps) + 1,)),
        ]
        + [pltpu.VMEM((beams, pulses, 2, keep), jnp.bfloat16) for keep in keeps],
        compiler_params=pltpu.CompilerParams(collective_id=0, has_side_effects=True),
    )(offsets, guard_cells, train_cells, scale_index, signal, replica)


def solution(mesh):
    placed = (
        P("beam", "pulse", None, "range"),
        P(None, ("beam", "pulse")),
        P("beam"),
        P("beam"),
        P("beam"),
        P("beam"),
    )
    sizes = (mesh.shape["beam"], mesh.shape["pulse"], mesh.shape["range"])
    return jax.shard_map(
        functools.partial(body, sizes),
        mesh=mesh,
        in_specs=placed,
        out_specs=(P("beam", "pulse", None, "range"), P("beam", "pulse", "range")),
        check_vma=False,
    )
```

```python
import functools

import jax
import jax.numpy as jnp
from jax import lax
from jax.experimental import pallas as pl
from jax.experimental.pallas import tpu as pltpu
from jax.sharding import PartitionSpec as P

TILE = 128
OFF_MAX = 128
EPSILON = 1e-06
GRANT = 24 << 20
MESH = pl.DeviceIdType.MESH


def plan(signal, replica, sizes):
    nb, npulse, nr = sizes
    pieces = nb * npulse
    piece = replica[1]
    gates = signal[3]
    total = gates * nr
    taps = min(piece * pieces, total)
    senders = -(-taps // piece)
    tiles = gates // TILE + 2
    panels = min(-(-piece * pieces // TILE) + 1, total // TILE)
    chunks = min(tiles + panels - 1, total // TILE + 1)
    beyond = (chunks - 1) * TILE - gates + OFF_MAX
    reach = min(-(-beyond // gates), nr - 1)
    keeps = [min(gates, beyond - s * gates) for s in range(reach)]
    return pieces, piece, gates, total, senders, tiles, panels, chunks, keeps


def gather(sizes, dims, *refs):
    pieces, piece, gates, total, senders, tiles, panels, chunks, keeps = dims
    nb, npulse, nr = sizes
    numbers, (sig, rep) = refs[:4], refs[4:6]
    hout, xa, weights, counts, factors = refs[6:11]
    hbuf, own, left, xf, yf = refs[11:16]
    offsets, guards, trains, scales = refs[16:20]
    here, hsend, hrecv, xsend, xrecv = refs[20:25]
    right = refs[25:]
    beams, pulses = sig.shape[0], sig.shape[1]
    rows = beams * pulses
    bi, pi, ri = lax.axis_index("beam"), lax.axis_index("pulse"), lax.axis_index("range")
    me = bi * npulse + pi
    reach = len(keeps)

    def where_is(index):
        return {"beam": index // npulse, "pulse": index % npulse}

    barrier = pltpu.get_barrier_semaphore()
    for s in range(senders):

        @pl.when(me != s)
        def _():
            pl.semaphore_signal(
                barrier, inc=1, device_id=where_is(s), device_id_type=MESH
            )

    for s in range(1, reach + 1):

        @pl.when(ri + s < nr)
        def _():
            pl.semaphore_signal(
                barrier, inc=1, device_id={"range": ri + s}, device_id_type=MESH
            )

    @pl.when(ri >= 1)
    def _():
        pl.semaphore_signal(
            barrier, inc=1, device_id={"range": ri - 1}, device_id_type=MESH
        )

    local = [pltpu.make_async_copy(sig, own, here.at[0])]
    for n, (number, kept) in enumerate(zip(numbers, (offsets, guards, trains, scales))):
        local.append(pltpu.make_async_copy(number, kept, here.at[n + 1]))
    for copy in local:
        copy.start()

    def head_copy(s):
        return pltpu.make_async_remote_copy(
            src_ref=sig.at[:, :, :, pl.ds(0, keeps[s - 1])],
            dst_ref=right[s - 1],
            send_sem=xsend.at[s],
            recv_sem=xrecv.at[s],
            device_id={"range": ri - s},
            device_id_type=MESH,
        )

    def tail_copy():
        return pltpu.make_async_remote_copy(
            src_ref=sig.at[:, :, :, pl.ds(gates - TILE, TILE)],
            dst_ref=left,
            send_sem=xsend.at[0],
            recv_sem=xrecv.at[0],
            device_id={"range": ri + 1},
            device_id_type=MESH,
        )

    def tap_copy(slot, step, target):
        return pltpu.make_async_remote_copy(
            src_ref=rep,
            dst_ref=hbuf.at[slot],
            send_sem=hsend.at[step],
            recv_sem=hrecv.at[slot],
            device_id=where_is(target),
            device_id_type=MESH,
        )

    expect = jnp.minimum(ri, reach) + jnp.where(ri + 1 < nr, 1, 0)
    pl.semaphore_wait(barrier, expect + jnp.where(me < senders, pieces - 1, 0))

    @pl.when(me < senders)
    def _():
        for step in range(pieces - 1, 0, -1):
            tap_copy(me, step, lax.rem(me + step, pieces)).start()

    for s in range(1, reach + 1):

        @pl.when(ri - s >= 0)
        def _():
            head_copy(s).start()

    @pl.when(ri + 1 < nr)
    def _():
        tail_copy().start()

    def own_taps():
        return pltpu.make_async_copy(rep, hbuf.at[me], here.at[5])

    @pl.when(me < senders)
    def _():
        own_taps().start()

    def place(source, start, width):
        for b in range(beams):
            for p in range(pulses):
                at = 2 * (b * pulses + p)
                pair = source[b, p].astype(jnp.float32)
                for c in range(width // TILE):
                    xf[start // TILE + c, at : at + 2, :] = pair[:, c * TILE : (c + 1) * TILE]

    def clear(start, stop):
        for c in range(start // TILE, stop // TILE):
            xf[c] = jnp.zeros((2 * rows, TILE), jnp.float32)

    for copy in local:
        copy.wait()
    place(own, TILE, gates)
    tail = TILE + gates + sum(keeps)
    width = yf.shape[1]
    clear(tail, width)

    lane = lax.broadcasted_iota(jnp.int32, (TILE, 3 * TILE), 1)
    row = lax.broadcasted_iota(jnp.int32, (TILE, 3 * TILE), 0)
    apart = jnp.abs(lane - TILE - row)
    position = ri * gates + lax.broadcasted_iota(jnp.int32, (pulses, gates), 1)
    for b in range(beams):
        guard, train = guards[b], trains[b]
        inside = (apart > guard) & (apart <= guard + train)
        weights[b] = jnp.where(inside, 1.0, 0.0).astype(jnp.bfloat16)
        count = jnp.clip(position - guard, 0, train) + jnp.clip(
            total - 1 - position - guard, 0, train
        )
        counts[b] = count.astype(jnp.float32)
        level = jnp.full((pulses, TILE), scales[b], jnp.int32).astype(jnp.float32)
        factors[b] = jnp.exp2(level / 8.0)

    @pl.when(ri >= 1)
    def _():
        tail_copy().wait_recv()
        place(left, 0, TILE)

    @pl.when(ri == 0)
    def _():
        clear(0, TILE)

    at = TILE + gates
    for s in range(1, reach + 1):
        start, keep = at, keeps[s - 1]

        @pl.when(ri + s < nr)
        def _():
            head_copy(s).wait_recv()
            place(right[s - 1], start, keep)

        @pl.when(ri + s >= nr)
        def _():
            clear(start, start + keep)

        at += keep

    for b in range(beams):
        low = 2 * b * pulses
        real, imag = [
            pltpu.roll(
                jnp.concatenate(
                    [
                        xf[c, pl.ds(low + part, pulses, stride=2), :]
                        for c in range(width // TILE)
                    ],
                    axis=1,
                ),
                width - offsets[b],
                1,
            )
            for part in range(2)
        ]
        yf[b * pulses : (b + 1) * pulses, :] = real
        yf[rows + b * pulses : rows + (b + 1) * pulses, :] = imag
    for c in range(chunks):
        real = yf[:rows, c * TILE : (c + 1) * TILE]
        imag = yf[rows:, c * TILE : (c + 1) * TILE]
        first = jnp.concatenate([real, imag], axis=1)
        second = jnp.concatenate([imag, -real], axis=1)
        xa[c] = jnp.concatenate([first, second], axis=0).astype(jnp.bfloat16)

    @pl.when(me < senders)
    def _():
        own_taps().wait()

    for s in range(senders):

        @pl.when(me != s)
        def _():
            tap_copy(s, 0, me).wait_recv()

    hout[...] = hbuf[...]

    @pl.when(me < senders)
    def _():
        for step in range(1, pieces):
            tap_copy(me, step, me).wait_send()

    for s in range(1, reach + 1):

        @pl.when(ri - s >= 0)
        def _():
            head_copy(s).wait_send()

    @pl.when(ri + 1 < nr)
    def _():
        tail_copy().wait_send()


def compute(sizes, dims, taps_ref, xa, weights, counts, factors, comp, ratio, xf):
    pieces, piece, gates, total, senders, tiles, panels, chunks, keeps = dims
    beams, pulses = comp.shape[0], comp.shape[1]
    rows = beams * pulses
    ri = lax.axis_index("range")

    across = tiles - 2

    per = TILE // piece if piece < TILE else 1
    spread = max(piece // TILE, 1)

    def taps_of(c):
        if piece >= TILE:
            return taps_ref[c // spread].astype(jnp.float32)[
                :, (c % spread) * TILE : (c % spread + 1) * TILE
            ]
        parts = [taps_ref[c * per + i].astype(jnp.float32) for i in range(per)]
        return jnp.concatenate(parts, axis=1)

    held = min(panels, (senders * piece) // TILE)
    lane = lax.broadcasted_iota(jnp.int32, (TILE, TILE), 1)
    row = lax.broadcasted_iota(jnp.int32, (TILE, TILE), 0)
    ahead = lane >= row

    def skewed(values):
        flat = jnp.broadcast_to(values, (TILE, TILE))
        return pltpu.roll(flat, 0, 1, stride=1, stride_axis=0)

    zero = jnp.zeros((TILE, TILE), jnp.float32)
    before = (zero, zero)
    sums = [None] * tiles
    for c in range(panels):
        if c < held:
            taps = taps_of(c)
            now = (skewed(taps[0:1]), skewed(taps[1:2]))
        else:
            now = (zero, zero)
        panel = jnp.concatenate(
            [jnp.where(ahead, n, b) for n, b in zip(now, before)], axis=1
        ).astype(jnp.bfloat16)
        before = now
        n = min(tiles, chunks - c)
        left_side = xa[c : c + n].reshape(n * 2 * rows, 2 * TILE)
        product = lax.dot_general(
            left_side, panel, (((1,), (1,)), ((), ())), preferred_element_type=jnp.float32
        )
        for i in range(n):
            part = product[i * 2 * rows : (i + 1) * 2 * rows]
            sums[i] = part if sums[i] is None else sums[i] + part

    powers = []
    for i in range(tiles):
        rounded = sums[i].astype(jnp.bfloat16).astype(jnp.float32)
        real, imag = rounded[:rows], rounded[rows:]
        power = real * real + imag * imag
        if i == 0:
            power = jnp.where(ri >= 1, power, 0.0)
        powers.append(power)
        if 1 <= i <= across:
            xf[i - 1, pl.ds(0, rows, stride=2), :] = real
            xf[i - 1, pl.ds(1, rows, stride=2), :] = imag
    for b in range(beams):
        for p in range(pulses):
            at = 2 * (b * pulses + p)
            for i in range(across):
                comp[b, p, :, i * TILE : (i + 1) * TILE] = xf[i, at : at + 2, :].astype(
                    jnp.bfloat16
                )

    split = []
    for power in powers:
        high = power.astype(jnp.bfloat16)
        rest = power - high.astype(jnp.float32)
        middle = rest.astype(jnp.bfloat16)
        low = (rest - middle.astype(jnp.float32)).astype(jnp.bfloat16)
        split.append([v.astype(jnp.float32) for v in (high, middle, low)])
    for b in range(beams):
        mine = slice(b * pulses, (b + 1) * pulses)
        side = jnp.concatenate(
            [
                jnp.concatenate([split[i + d][k][mine] for d in range(3)], axis=1)
                for i in range(across)
                for k in range(3)
            ],
            axis=0,
        ).astype(jnp.bfloat16)
        window = lax.dot_general(
            side, weights[b], (((1,), (1,)), ((), ())), preferred_element_type=jnp.float32
        )
        for i in range(across):
            base = 3 * i * pulses
            noise = (
                window[base : base + pulses]
                + window[base + pulses : base + 2 * pulses]
                + window[base + 2 * pulses : base + 3 * pulses]
            ) / counts[b, :, i * TILE : (i + 1) * TILE]
            ratio[b, :, i * TILE : (i + 1) * TILE] = powers[i + 1][mine] / (
                factors[b] * (noise + EPSILON)
            )


def body(sizes, signal, replica, guard_cells, train_cells, scale_index, offsets):
    dims = plan(signal.shape, replica.shape, sizes)
    pieces, piece, gates, total, senders, tiles, panels, chunks, keeps = dims
    beams, pulses = signal.shape[0], signal.shape[1]
    rows = beams * pulses
    width = max(chunks * TILE + OFF_MAX, TILE + gates + sum(keeps))
    vmem = pl.BlockSpec(memory_space=pltpu.VMEM)
    placed = pl.BlockSpec(memory_space=pltpu.HBM)
    reach = len(keeps)
    operands = (offsets, guard_cells, train_cells, scale_index, signal, replica)
    gathered = pl.pallas_call(
        functools.partial(gather, sizes, dims),
        out_shape=(
            jax.ShapeDtypeStruct((senders, 2, piece), jnp.bfloat16),
            jax.ShapeDtypeStruct((chunks, 2 * rows, 2 * TILE), jnp.bfloat16),
            jax.ShapeDtypeStruct((beams, TILE, 3 * TILE), jnp.bfloat16),
            jax.ShapeDtypeStruct((beams, pulses, gates), jnp.float32),
            jax.ShapeDtypeStruct((beams, pulses, TILE), jnp.float32),
        ),
        in_specs=[placed] * 6,
        out_specs=(vmem,) * 5,
        scratch_shapes=[
            pltpu.VMEM((senders, 2, piece), jnp.bfloat16),
            pltpu.VMEM(signal.shape, jnp.bfloat16),
            pltpu.VMEM((beams, pulses, 2, TILE), jnp.bfloat16),
            pltpu.VMEM((width // TILE, 2 * rows, TILE), jnp.float32),
            pltpu.VMEM((2 * rows, width), jnp.float32),
        ]
        + [pltpu.SMEM((beams,), jnp.int32)] * 4
        + [
            pltpu.SemaphoreType.DMA((6,)),
            pltpu.SemaphoreType.DMA((pieces,)),
            pltpu.SemaphoreType.DMA((senders,)),
            pltpu.SemaphoreType.DMA((reach + 1,)),
            pltpu.SemaphoreType.DMA((reach + 1,)),
        ]
        + [pltpu.VMEM((beams, pulses, 2, keep), jnp.bfloat16) for keep in keeps],
        compiler_params=pltpu.CompilerParams(
            collective_id=0, has_side_effects=True, vmem_limit_bytes=GRANT
        ),
        name="gather",
    )(*[pltpu.with_memory_space_constraint(v, pltpu.HBM) for v in operands])
    return pl.pallas_call(
        functools.partial(compute, sizes, dims),
        out_shape=(
            jax.ShapeDtypeStruct(signal.shape, jnp.bfloat16),
            jax.ShapeDtypeStruct((beams, pulses, gates), jnp.float32),
        ),
        in_specs=[vmem] * 5,
        out_specs=(vmem, vmem),
        scratch_shapes=[pltpu.VMEM((gates // TILE, 2 * rows, TILE), jnp.float32)],
        compiler_params=pltpu.CompilerParams(vmem_limit_bytes=GRANT),
        name="compute",
    )(*gathered)


def solution(mesh):
    placed = (
        P("beam", "pulse", None, "range"),
        P(None, ("beam", "pulse")),
        P("beam"),
        P("beam"),
        P("beam"),
        P("beam"),
    )
    sizes = (mesh.shape["beam"], mesh.shape["pulse"], mesh.shape["range"])
    return jax.shard_map(
        functools.partial(body, sizes),
        mesh=mesh,
        in_specs=placed,
        out_specs=(P("beam", "pulse", None, "range"), P("beam", "pulse", "range")),
        check_vma=False,
    )
```

```python
import functools

import jax
import jax.numpy as jnp
from jax import lax
from jax.experimental import pallas as pl
from jax.experimental.pallas import tpu as pltpu
from jax.sharding import PartitionSpec as P

TILE = 128
OFF_MAX = 128
EPSILON = 1e-06
GRANT = 24 << 20
MESH = pl.DeviceIdType.MESH


def plan(signal, replica, sizes):
    nb, npulse, nr = sizes
    pieces = nb * npulse
    piece = replica[1]
    gates = signal[3]
    total = gates * nr
    taps = min(piece * pieces, total)
    senders = -(-taps // (piece * npulse)) * npulse
    tiles = gates // TILE + 2
    panels = min(-(-piece * pieces // TILE) + 1, total // TILE)
    chunks = min(tiles + panels - 1, total // TILE + 1)
    beyond = (chunks - 1) * TILE - gates + OFF_MAX
    reach = min(-(-beyond // gates), nr - 1)
    keeps = [min(gates, beyond - s * gates) for s in range(reach)]
    return pieces, piece, gates, total, senders, tiles, panels, chunks, keeps


def gather(sizes, dims, *refs):
    pieces, piece, gates, total, senders, tiles, panels, chunks, keeps = dims
    nb, npulse, nr = sizes
    numbers, (sig, rep) = refs[:4], refs[4:6]
    hout, xa, weights, counts, factors = refs[6:11]
    hbuf, own, left, xf, yf = refs[11:16]
    offsets, guards, trains, scales = refs[16:20]
    here, hsend, hrecv, xsend, xrecv, ready = refs[20:26]
    right = refs[26:]
    beams, pulses = sig.shape[0], sig.shape[1]
    rows = beams * pulses
    bi, pi, ri = lax.axis_index("beam"), lax.axis_index("pulse"), lax.axis_index("range")
    me = bi * npulse + pi
    planes = senders // npulse
    reach = len(keeps)

    def say(semaphore, plane, pulse):
        pl.semaphore_signal(
            semaphore,
            inc=1,
            device_id={"beam": plane, "pulse": pulse},
            device_id_type=MESH,
        )

    barrier = pltpu.get_barrier_semaphore()

    @pl.when(bi + 1 < nb)
    def _():
        for j in range(npulse):
            say(barrier, bi + 1, j)

    @pl.when(bi < planes)
    def _():
        for j in range(1, npulse):
            say(barrier, bi, lax.rem(pi + j, npulse))

    for s in range(1, reach + 1):

        @pl.when(ri + s < nr)
        def _():
            pl.semaphore_signal(
                barrier, inc=1, device_id={"range": ri + s}, device_id_type=MESH
            )

    @pl.when(ri >= 1)
    def _():
        pl.semaphore_signal(
            barrier, inc=1, device_id={"range": ri - 1}, device_id_type=MESH
        )

    local = [pltpu.make_async_copy(sig, own, here.at[0])]
    for n, (number, kept) in enumerate(zip(numbers, (offsets, guards, trains, scales))):
        local.append(pltpu.make_async_copy(number, kept, here.at[n + 1]))
    for copy in local:
        copy.start()

    def head_copy(s):
        return pltpu.make_async_remote_copy(
            src_ref=sig.at[:, :, :, pl.ds(0, keeps[s - 1])],
            dst_ref=right[s - 1],
            send_sem=xsend.at[s],
            recv_sem=xrecv.at[s],
            device_id={"range": ri - s},
            device_id_type=MESH,
        )

    def tail_copy():
        return pltpu.make_async_remote_copy(
            src_ref=sig.at[:, :, :, pl.ds(gates - TILE, TILE)],
            dst_ref=left,
            send_sem=xsend.at[0],
            recv_sem=xrecv.at[0],
            device_id={"range": ri + 1},
            device_id_type=MESH,
        )

    def tap_copies(source, slot, way, plane):
        return [
            pltpu.make_async_remote_copy(
                src_ref=source,
                dst_ref=hbuf.at[slot],
                send_sem=hsend.at[way, j],
                recv_sem=hrecv.at[slot],
                device_id={"beam": plane, "pulse": lax.rem(pi + j, npulse)},
                device_id_type=MESH,
            )
            for j in range(1 if way == 0 else 0, npulse)
        ]

    def same_plane():
        return tap_copies(rep, me, 0, bi)

    def down(b, source):
        return tap_copies(source, b * npulse + pi, 1 + b, bi - 1)

    def up(b, source):
        return tap_copies(source, b * npulse + pi, 1 + planes + b, bi + 1)

    expect = jnp.minimum(ri, reach) + jnp.where(ri + 1 < nr, 1, 0)
    expect += jnp.where(bi < planes, npulse - 1, 0) + jnp.where(bi >= 1, npulse, 0)
    pl.semaphore_wait(barrier, expect)

    @pl.when(bi >= 1)
    def _():
        for j in range(npulse):
            say(ready, bi - 1, lax.rem(pi + j, npulse))

    for b in range(planes):

        @pl.when((bi == b) & (bi >= 1))
        def _():
            for copy in down(b, rep):
                copy.start()

    @pl.when(bi < planes)
    def _():
        for copy in same_plane():
            copy.start()

    for s in range(1, reach + 1):

        @pl.when(ri - s >= 0)
        def _():
            head_copy(s).start()

    @pl.when(ri + 1 < nr)
    def _():
        tail_copy().start()

    def own_taps():
        return pltpu.make_async_copy(rep, hbuf.at[me], here.at[5])

    @pl.when(me < senders)
    def _():
        own_taps().start()

    def place(source, start, width):
        for b in range(beams):
            for p in range(pulses):
                at = 2 * (b * pulses + p)
                pair = source[b, p].astype(jnp.float32)
                for c in range(width // TILE):
                    xf[start // TILE + c, at : at + 2, :] = pair[:, c * TILE : (c + 1) * TILE]

    def clear(start, stop):
        for c in range(start // TILE, stop // TILE):
            xf[c] = jnp.zeros((2 * rows, TILE), jnp.float32)

    for copy in local:
        copy.wait()
    place(own, TILE, gates)
    tail = TILE + gates + sum(keeps)
    width = yf.shape[1]
    clear(tail, width)

    lane = lax.broadcasted_iota(jnp.int32, (TILE, 3 * TILE), 1)
    row = lax.broadcasted_iota(jnp.int32, (TILE, 3 * TILE), 0)
    apart = jnp.abs(lane - TILE - row)
    position = ri * gates + lax.broadcasted_iota(jnp.int32, (pulses, gates), 1)
    for b in range(beams):
        guard, train = guards[b], trains[b]
        inside = (apart > guard) & (apart <= guard + train)
        weights[b] = jnp.where(inside, 1.0, 0.0).astype(jnp.bfloat16)
        count = jnp.clip(position - guard, 0, train) + jnp.clip(
            total - 1 - position - guard, 0, train
        )
        counts[b] = count.astype(jnp.float32)
        level = jnp.full((pulses, TILE), scales[b], jnp.int32).astype(jnp.float32)
        factors[b] = jnp.exp2(level / 8.0)

    @pl.when(bi + 1 < nb)
    def _():
        pl.semaphore_wait(ready, npulse)
        for b in range(planes):

            @pl.when(bi == b)
            def _():
                for copy in up(b, rep):
                    copy.start()

    @pl.when(ri >= 1)
    def _():
        tail_copy().wait_recv()
        place(left, 0, TILE)

    @pl.when(ri == 0)
    def _():
        clear(0, TILE)

    at = TILE + gates
    for s in range(1, reach + 1):
        start, keep = at, keeps[s - 1]

        @pl.when(ri + s < nr)
        def _():
            head_copy(s).wait_recv()
            place(right[s - 1], start, keep)

        @pl.when(ri + s >= nr)
        def _():
            clear(start, start + keep)

        at += keep

    for b in range(beams):
        low = 2 * b * pulses
        real, imag = [
            pltpu.roll(
                jnp.concatenate(
                    [
                        xf[c, pl.ds(low + part, pulses, stride=2), :]
                        for c in range(width // TILE)
                    ],
                    axis=1,
                ),
                width - offsets[b],
                1,
            )
            for part in range(2)
        ]
        yf[b * pulses : (b + 1) * pulses, :] = real
        yf[rows + b * pulses : rows + (b + 1) * pulses, :] = imag
    for c in range(chunks):
        real = yf[:rows, c * TILE : (c + 1) * TILE]
        imag = yf[rows:, c * TILE : (c + 1) * TILE]
        first = jnp.concatenate([real, imag], axis=1)
        second = jnp.concatenate([imag, -real], axis=1)
        xa[c] = jnp.concatenate([first, second], axis=0).astype(jnp.bfloat16)

    @pl.when(me < senders)
    def _():
        own_taps().wait()

    for b in reversed(range(planes)):

        @pl.when(bi != b)
        def _():
            slot = b * npulse + pi
            up(b, hbuf.at[slot])[0].wait_recv()

            @pl.when((bi < b) & (bi >= 1))
            def _():
                for copy in down(b, hbuf.at[slot]):
                    copy.start()

            @pl.when((bi > b) & (bi + 1 < nb))
            def _():
                for copy in up(b, hbuf.at[slot]):
                    copy.start()

    for slot in range(senders):

        @pl.when(pi != slot % npulse)
        def _():
            tap_copies(rep, slot, 1, 0)[0].wait_recv()

    hout[...] = hbuf[...]

    @pl.when(me < senders)
    def _():
        for copy in same_plane():
            copy.wait_send()

    for b in range(planes):

        @pl.when((bi <= b) & (bi >= 1))
        def _():
            for copy in down(b, rep):
                copy.wait_send()

        @pl.when((bi >= b) & (bi + 1 < nb))
        def _():
            for copy in up(b, rep):
                copy.wait_send()

    for s in range(1, reach + 1):

        @pl.when(ri - s >= 0)
        def _():
            head_copy(s).wait_send()

    @pl.when(ri + 1 < nr)
    def _():
        tail_copy().wait_send()


def compute(sizes, dims, taps_ref, xa, weights, counts, factors, comp, ratio, xf):
    pieces, piece, gates, total, senders, tiles, panels, chunks, keeps = dims
    beams, pulses = comp.shape[0], comp.shape[1]
    rows = beams * pulses
    ri = lax.axis_index("range")

    across = tiles - 2

    per = TILE // piece if piece < TILE else 1
    spread = max(piece // TILE, 1)

    def taps_of(c):
        if piece >= TILE:
            return taps_ref[c // spread].astype(jnp.float32)[
                :, (c % spread) * TILE : (c % spread + 1) * TILE
            ]
        parts = [taps_ref[c * per + i].astype(jnp.float32) for i in range(per)]
        return jnp.concatenate(parts, axis=1)

    held = min(panels, (senders * piece) // TILE)
    lane = lax.broadcasted_iota(jnp.int32, (TILE, TILE), 1)
    row = lax.broadcasted_iota(jnp.int32, (TILE, TILE), 0)
    ahead = lane >= row

    def skewed(values):
        flat = jnp.broadcast_to(values, (TILE, TILE))
        return pltpu.roll(flat, 0, 1, stride=1, stride_axis=0)

    zero = jnp.zeros((TILE, TILE), jnp.float32)
    before = (zero, zero)
    sums = [None] * tiles
    for c in range(panels):
        if c < held:
            taps = taps_of(c)
            now = (skewed(taps[0:1]), skewed(taps[1:2]))
        else:
            now = (zero, zero)
        panel = jnp.concatenate(
            [jnp.where(ahead, n, b) for n, b in zip(now, before)], axis=1
        ).astype(jnp.bfloat16)
        before = now
        n = min(tiles, chunks - c)
        left_side = xa[c : c + n].reshape(n * 2 * rows, 2 * TILE)
        product = lax.dot_general(
            left_side, panel, (((1,), (1,)), ((), ())), preferred_element_type=jnp.float32
        )
        for i in range(n):
            part = product[i * 2 * rows : (i + 1) * 2 * rows]
            sums[i] = part if sums[i] is None else sums[i] + part

    powers = []
    for i in range(tiles):
        rounded = sums[i].astype(jnp.bfloat16).astype(jnp.float32)
        real, imag = rounded[:rows], rounded[rows:]
        power = real * real + imag * imag
        if i == 0:
            power = jnp.where(ri >= 1, power, 0.0)
        powers.append(power)
        if 1 <= i <= across:
            xf[i - 1, pl.ds(0, rows, stride=2), :] = real
            xf[i - 1, pl.ds(1, rows, stride=2), :] = imag
    for b in range(beams):
        for p in range(pulses):
            at = 2 * (b * pulses + p)
            for i in range(across):
                comp[b, p, :, i * TILE : (i + 1) * TILE] = xf[i, at : at + 2, :].astype(
                    jnp.bfloat16
                )

    split = []
    for power in powers:
        high = power.astype(jnp.bfloat16)
        rest = power - high.astype(jnp.float32)
        middle = rest.astype(jnp.bfloat16)
        low = (rest - middle.astype(jnp.float32)).astype(jnp.bfloat16)
        split.append([v.astype(jnp.float32) for v in (high, middle, low)])
    for b in range(beams):
        mine = slice(b * pulses, (b + 1) * pulses)
        side = jnp.concatenate(
            [
                jnp.concatenate([split[i + d][k][mine] for d in range(3)], axis=1)
                for i in range(across)
                for k in range(3)
            ],
            axis=0,
        ).astype(jnp.bfloat16)
        window = lax.dot_general(
            side, weights[b], (((1,), (1,)), ((), ())), preferred_element_type=jnp.float32
        )
        for i in range(across):
            base = 3 * i * pulses
            noise = (
                window[base : base + pulses]
                + window[base + pulses : base + 2 * pulses]
                + window[base + 2 * pulses : base + 3 * pulses]
            ) / counts[b, :, i * TILE : (i + 1) * TILE]
            ratio[b, :, i * TILE : (i + 1) * TILE] = powers[i + 1][mine] / (
                factors[b] * (noise + EPSILON)
            )


def body(sizes, signal, replica, guard_cells, train_cells, scale_index, offsets):
    dims = plan(signal.shape, replica.shape, sizes)
    pieces, piece, gates, total, senders, tiles, panels, chunks, keeps = dims
    beams, pulses = signal.shape[0], signal.shape[1]
    rows = beams * pulses
    width = max(chunks * TILE + OFF_MAX, TILE + gates + sum(keeps))
    vmem = pl.BlockSpec(memory_space=pltpu.VMEM)
    placed = pl.BlockSpec(memory_space=pltpu.HBM)
    reach = len(keeps)
    operands = (offsets, guard_cells, train_cells, scale_index, signal, replica)
    gathered = pl.pallas_call(
        functools.partial(gather, sizes, dims),
        out_shape=(
            jax.ShapeDtypeStruct((senders, 2, piece), jnp.bfloat16),
            jax.ShapeDtypeStruct((chunks, 2 * rows, 2 * TILE), jnp.bfloat16),
            jax.ShapeDtypeStruct((beams, TILE, 3 * TILE), jnp.bfloat16),
            jax.ShapeDtypeStruct((beams, pulses, gates), jnp.float32),
            jax.ShapeDtypeStruct((beams, pulses, TILE), jnp.float32),
        ),
        in_specs=[placed] * 6,
        out_specs=(vmem,) * 5,
        scratch_shapes=[
            pltpu.VMEM((senders, 2, piece), jnp.bfloat16),
            pltpu.VMEM(signal.shape, jnp.bfloat16),
            pltpu.VMEM((beams, pulses, 2, TILE), jnp.bfloat16),
            pltpu.VMEM((width // TILE, 2 * rows, TILE), jnp.float32),
            pltpu.VMEM((2 * rows, width), jnp.float32),
        ]
        + [pltpu.SMEM((beams,), jnp.int32)] * 4
        + [
            pltpu.SemaphoreType.DMA((6,)),
            pltpu.SemaphoreType.DMA((2 * (senders // sizes[1]) + 1, sizes[1])),
            pltpu.SemaphoreType.DMA((senders,)),
            pltpu.SemaphoreType.DMA((reach + 1,)),
            pltpu.SemaphoreType.DMA((reach + 1,)),
            pltpu.SemaphoreType.REGULAR,
        ]
        + [pltpu.VMEM((beams, pulses, 2, keep), jnp.bfloat16) for keep in keeps],
        compiler_params=pltpu.CompilerParams(
            collective_id=0, has_side_effects=True, vmem_limit_bytes=GRANT
        ),
        name="gather",
    )(*[pltpu.with_memory_space_constraint(v, pltpu.HBM) for v in operands])
    return pl.pallas_call(
        functools.partial(compute, sizes, dims),
        out_shape=(
            jax.ShapeDtypeStruct(signal.shape, jnp.bfloat16),
            jax.ShapeDtypeStruct((beams, pulses, gates), jnp.float32),
        ),
        in_specs=[vmem] * 5,
        out_specs=(vmem, vmem),
        scratch_shapes=[pltpu.VMEM((gates // TILE, 2 * rows, TILE), jnp.float32)],
        compiler_params=pltpu.CompilerParams(vmem_limit_bytes=GRANT),
        name="compute",
    )(*gathered)


def solution(mesh):
    placed = (
        P("beam", "pulse", None, "range"),
        P(None, ("beam", "pulse")),
        P("beam"),
        P("beam"),
        P("beam"),
        P("beam"),
    )
    sizes = (mesh.shape["beam"], mesh.shape["pulse"], mesh.shape["range"])
    return jax.shard_map(
        functools.partial(body, sizes),
        mesh=mesh,
        in_specs=placed,
        out_specs=(P("beam", "pulse", None, "range"), P("beam", "pulse", "range")),
        check_vma=False,
    )
```

```python
import functools

import jax
import jax.numpy as jnp
from jax import lax
from jax.experimental import pallas as pl
from jax.experimental.pallas import tpu as pltpu
from jax.sharding import PartitionSpec as P

TILE = 128
OFF_MAX = 128
EPSILON = 1e-06
GRANT = 24 << 20
MESH = pl.DeviceIdType.MESH


def plan(signal, replica, sizes):
    nb, npulse, nr = sizes
    pieces = nb * npulse
    piece = replica[1]
    gates = signal[3]
    total = gates * nr
    taps = min(piece * pieces, total)
    senders = -(-taps // (piece * npulse)) * npulse
    tiles = gates // TILE + 2
    panels = min(-(-piece * pieces // TILE) + 1, total // TILE)
    chunks = min(tiles + panels - 1, total // TILE + 1)
    beyond = (chunks - 1) * TILE - gates + OFF_MAX
    reach = min(-(-beyond // gates), nr - 1)
    keeps = [min(gates, beyond - s * gates) for s in range(reach)]
    return pieces, piece, gates, total, senders, tiles, panels, chunks, keeps


def gather(sizes, dims, *refs):
    pieces, piece, gates, total, senders, tiles, panels, chunks, keeps = dims
    nb, npulse, nr = sizes
    numbers, (sig, rep) = refs[:4], refs[4:6]
    hout, xa, weights, counts, factors = refs[6:11]
    hbuf, own, left, xf, yf = refs[11:16]
    offsets, guards, trains, scales = refs[16:20]
    here, hsend, hrecv, xsend, xrecv, ready = refs[20:26]
    right = refs[26:]
    beams, pulses = sig.shape[0], sig.shape[1]
    rows = beams * pulses
    bi, pi, ri = lax.axis_index("beam"), lax.axis_index("pulse"), lax.axis_index("range")
    me = bi * npulse + pi
    planes = senders // npulse
    reach = len(keeps)

    def say(semaphore, plane, pulse):
        pl.semaphore_signal(
            semaphore,
            inc=1,
            device_id={"beam": plane, "pulse": pulse},
            device_id_type=MESH,
        )

    barrier = pltpu.get_barrier_semaphore()

    @pl.when(bi < planes)
    def _():
        for j in range(1, npulse):
            say(barrier, bi, lax.rem(pi + j, npulse))

    for side in (-1, 1):

        @pl.when((bi < planes) & (bi + side >= 0) & (bi + side < planes))
        def _():
            for j in range(npulse):
                say(barrier, bi + side, lax.rem(pi + j, npulse))

    @pl.when(bi == planes - 1)
    def _():
        for q in range(planes, nb):
            for j in range(npulse):
                say(barrier, q, lax.rem(pi + j, npulse))

    for s in range(1, reach + 1):

        @pl.when(ri + s < nr)
        def _():
            pl.semaphore_signal(
                barrier, inc=1, device_id={"range": ri + s}, device_id_type=MESH
            )

    @pl.when(ri >= 1)
    def _():
        pl.semaphore_signal(
            barrier, inc=1, device_id={"range": ri - 1}, device_id_type=MESH
        )

    local = [pltpu.make_async_copy(sig, own, here.at[0])]
    for n, (number, kept) in enumerate(zip(numbers, (offsets, guards, trains, scales))):
        local.append(pltpu.make_async_copy(number, kept, here.at[n + 1]))
    for copy in local:
        copy.start()

    def head_copy(s):
        return pltpu.make_async_remote_copy(
            src_ref=sig.at[:, :, :, pl.ds(0, keeps[s - 1])],
            dst_ref=right[s - 1],
            send_sem=xsend.at[s],
            recv_sem=xrecv.at[s],
            device_id={"range": ri - s},
            device_id_type=MESH,
        )

    def tail_copy():
        return pltpu.make_async_remote_copy(
            src_ref=sig.at[:, :, :, pl.ds(gates - TILE, TILE)],
            dst_ref=left,
            send_sem=xsend.at[0],
            recv_sem=xrecv.at[0],
            device_id={"range": ri + 1},
            device_id_type=MESH,
        )

    def tap_copies(source, slot, way, plane):
        return [
            pltpu.make_async_remote_copy(
                src_ref=source,
                dst_ref=hbuf.at[slot],
                send_sem=hsend.at[way, j],
                recv_sem=hrecv.at[slot],
                device_id={"beam": plane, "pulse": lax.rem(pi + j, npulse)},
                device_id_type=MESH,
            )
            for j in range(1 if way == 0 else 0, npulse)
        ]

    def same_plane():
        return tap_copies(rep, me, 0, bi)

    def down(b, source):
        return tap_copies(source, b * npulse + pi, 1 + b, bi - 1)

    def up(b, source):
        return tap_copies(source, b * npulse + pi, 1 + planes + b, bi + 1)

    def beyond(b, source, q):
        way = 1 + (2 + q - planes) * planes + b
        return tap_copies(source, b * npulse + pi, way, q)

    def arrived(slot):
        copy = pltpu.make_async_remote_copy(
            src_ref=rep,
            dst_ref=hbuf.at[slot],
            send_sem=hsend.at[0, 0],
            recv_sem=hrecv.at[slot],
            device_id={"beam": bi},
            device_id_type=MESH,
        )
        copy.wait_recv()

    expect = jnp.minimum(ri, reach) + jnp.where(ri + 1 < nr, 1, 0)
    beside = jnp.where(bi >= 1, npulse, 0) + jnp.where(bi + 1 < planes, npulse, 0)
    expect += jnp.where(bi < planes, npulse - 1 + beside, npulse)
    pl.semaphore_wait(barrier, expect)

    for q in range(planes, nb):

        @pl.when(bi == q)
        def _():
            for j in range(npulse):
                say(ready.at[q - planes], planes - 1, lax.rem(pi + j, npulse))

    for b in range(planes):

        @pl.when(bi == b)
        def _():
            if b >= 1:
                for copy in down(b, rep):
                    copy.start()
            if b + 1 < planes:
                for copy in up(b, rep):
                    copy.start()
            for copy in same_plane():
                copy.start()

    for s in range(1, reach + 1):

        @pl.when(ri - s >= 0)
        def _():
            head_copy(s).start()

    @pl.when(ri + 1 < nr)
    def _():
        tail_copy().start()

    def own_taps():
        return pltpu.make_async_copy(rep, hbuf.at[me], here.at[5])

    @pl.when(me < senders)
    def _():
        own_taps().start()

    def place(source, start, width):
        for b in range(beams):
            for p in range(pulses):
                at = 2 * (b * pulses + p)
                pair = source[b, p].astype(jnp.float32)
                for c in range(width // TILE):
                    xf[start // TILE + c, at : at + 2, :] = pair[:, c * TILE : (c + 1) * TILE]

    def clear(start, stop):
        for c in range(start // TILE, stop // TILE):
            xf[c] = jnp.zeros((2 * rows, TILE), jnp.float32)

    for copy in local:
        copy.wait()
    place(own, TILE, gates)
    tail = TILE + gates + sum(keeps)
    width = yf.shape[1]
    clear(tail, width)

    lane = lax.broadcasted_iota(jnp.int32, (TILE, 3 * TILE), 1)
    row = lax.broadcasted_iota(jnp.int32, (TILE, 3 * TILE), 0)
    apart = jnp.abs(lane - TILE - row)
    position = ri * gates + lax.broadcasted_iota(jnp.int32, (pulses, gates), 1)
    for b in range(beams):
        guard, train = guards[b], trains[b]
        inside = (apart > guard) & (apart <= guard + train)
        weights[b] = jnp.where(inside, 1.0, 0.0).astype(jnp.bfloat16)
        count = jnp.clip(position - guard, 0, train) + jnp.clip(
            total - 1 - position - guard, 0, train
        )
        counts[b] = count.astype(jnp.float32)
        level = jnp.full((pulses, TILE), scales[b], jnp.int32).astype(jnp.float32)
        factors[b] = jnp.exp2(level / 8.0)

    for b in reversed(range(planes)):

        @pl.when((bi < planes) & (bi != b) & (bi >= 1))
        def _():
            slot = b * npulse + pi
            arrived(slot)

            @pl.when(bi < b)
            def _():
                for copy in down(b, hbuf.at[slot]):
                    copy.start()

            @pl.when((bi > b) & (bi + 1 < planes))
            def _():
                for copy in up(b, hbuf.at[slot]):
                    copy.start()

    @pl.when(bi == planes - 1)
    def _():
        for q in range(planes, nb):
            pl.semaphore_wait(ready.at[q - planes], npulse)
            for b in range(planes):
                source = rep if b == planes - 1 else hbuf.at[b * npulse + pi]
                for copy in beyond(b, source, q):
                    copy.start()

    @pl.when(ri >= 1)
    def _():
        tail_copy().wait_recv()
        place(left, 0, TILE)

    @pl.when(ri == 0)
    def _():
        clear(0, TILE)

    at = TILE + gates
    for s in range(1, reach + 1):
        start, keep = at, keeps[s - 1]

        @pl.when(ri + s < nr)
        def _():
            head_copy(s).wait_recv()
            place(right[s - 1], start, keep)

        @pl.when(ri + s >= nr)
        def _():
            clear(start, start + keep)

        at += keep

    for b in range(beams):
        low = 2 * b * pulses
        real, imag = [
            pltpu.roll(
                jnp.concatenate(
                    [
                        xf[c, pl.ds(low + part, pulses, stride=2), :]
                        for c in range(width // TILE)
                    ],
                    axis=1,
                ),
                width - offsets[b],
                1,
            )
            for part in range(2)
        ]
        yf[b * pulses : (b + 1) * pulses, :] = real
        yf[rows + b * pulses : rows + (b + 1) * pulses, :] = imag
    for c in range(chunks):
        real = yf[:rows, c * TILE : (c + 1) * TILE]
        imag = yf[rows:, c * TILE : (c + 1) * TILE]
        first = jnp.concatenate([real, imag], axis=1)
        second = jnp.concatenate([imag, -real], axis=1)
        xa[c] = jnp.concatenate([first, second], axis=0).astype(jnp.bfloat16)

    @pl.when(me < senders)
    def _():
        own_taps().wait()

    for slot in range(senders):

        first = (bi == 0) & (slot >= npulse)

        @pl.when((pi != slot % npulse) | (bi >= planes) | first)
        def _():
            arrived(slot)

    hout[...] = hbuf[...]

    @pl.when(bi < planes)
    def _():
        for copy in same_plane():
            copy.wait_send()

    for b in range(planes):

        @pl.when((bi < planes) & (bi <= b) & (bi >= 1))
        def _():
            for copy in down(b, rep):
                copy.wait_send()

        @pl.when((bi >= b) & (bi + 1 < planes))
        def _():
            for copy in up(b, rep):
                copy.wait_send()

    @pl.when(bi == planes - 1)
    def _():
        for q in range(planes, nb):
            for b in range(planes):
                for copy in beyond(b, rep, q):
                    copy.wait_send()

    for s in range(1, reach + 1):

        @pl.when(ri - s >= 0)
        def _():
            head_copy(s).wait_send()

    @pl.when(ri + 1 < nr)
    def _():
        tail_copy().wait_send()


def compute(sizes, dims, taps_ref, xa, weights, counts, factors, comp, ratio, xf):
    pieces, piece, gates, total, senders, tiles, panels, chunks, keeps = dims
    beams, pulses = comp.shape[0], comp.shape[1]
    rows = beams * pulses
    ri = lax.axis_index("range")

    across = tiles - 2

    per = TILE // piece if piece < TILE else 1
    spread = max(piece // TILE, 1)

    def taps_of(c):
        if piece >= TILE:
            return taps_ref[c // spread].astype(jnp.float32)[
                :, (c % spread) * TILE : (c % spread + 1) * TILE
            ]
        parts = [taps_ref[c * per + i].astype(jnp.float32) for i in range(per)]
        return jnp.concatenate(parts, axis=1)

    held = min(panels, (senders * piece) // TILE)
    lane = lax.broadcasted_iota(jnp.int32, (TILE, TILE), 1)
    row = lax.broadcasted_iota(jnp.int32, (TILE, TILE), 0)
    ahead = lane >= row

    def skewed(values):
        flat = jnp.broadcast_to(values, (TILE, TILE))
        return pltpu.roll(flat, 0, 1, stride=1, stride_axis=0)

    zero = jnp.zeros((TILE, TILE), jnp.float32)
    before = (zero, zero)
    sums = [None] * tiles
    for c in range(panels):
        if c < held:
            taps = taps_of(c)
            now = (skewed(taps[0:1]), skewed(taps[1:2]))
        else:
            now = (zero, zero)
        panel = jnp.concatenate(
            [jnp.where(ahead, n, b) for n, b in zip(now, before)], axis=1
        ).astype(jnp.bfloat16)
        before = now
        n = min(tiles, chunks - c)
        left_side = xa[c : c + n].reshape(n * 2 * rows, 2 * TILE)
        product = lax.dot_general(
            left_side, panel, (((1,), (1,)), ((), ())), preferred_element_type=jnp.float32
        )
        for i in range(n):
            part = product[i * 2 * rows : (i + 1) * 2 * rows]
            sums[i] = part if sums[i] is None else sums[i] + part

    powers = []
    for i in range(tiles):
        rounded = sums[i].astype(jnp.bfloat16).astype(jnp.float32)
        real, imag = rounded[:rows], rounded[rows:]
        power = real * real + imag * imag
        if i == 0:
            power = jnp.where(ri >= 1, power, 0.0)
        powers.append(power)
        if 1 <= i <= across:
            xf[i - 1, pl.ds(0, rows, stride=2), :] = real
            xf[i - 1, pl.ds(1, rows, stride=2), :] = imag
    for b in range(beams):
        for p in range(pulses):
            at = 2 * (b * pulses + p)
            for i in range(across):
                comp[b, p, :, i * TILE : (i + 1) * TILE] = xf[i, at : at + 2, :].astype(
                    jnp.bfloat16
                )

    split = []
    for power in powers:
        high = power.astype(jnp.bfloat16)
        rest = power - high.astype(jnp.float32)
        middle = rest.astype(jnp.bfloat16)
        low = (rest - middle.astype(jnp.float32)).astype(jnp.bfloat16)
        split.append([v.astype(jnp.float32) for v in (high, middle, low)])
    for b in range(beams):
        mine = slice(b * pulses, (b + 1) * pulses)
        side = jnp.concatenate(
            [
                jnp.concatenate([split[i + d][k][mine] for d in range(3)], axis=1)
                for i in range(across)
                for k in range(3)
            ],
            axis=0,
        ).astype(jnp.bfloat16)
        window = lax.dot_general(
            side, weights[b], (((1,), (1,)), ((), ())), preferred_element_type=jnp.float32
        )
        for i in range(across):
            base = 3 * i * pulses
            noise = (
                window[base : base + pulses]
                + window[base + pulses : base + 2 * pulses]
                + window[base + 2 * pulses : base + 3 * pulses]
            ) / counts[b, :, i * TILE : (i + 1) * TILE]
            ratio[b, :, i * TILE : (i + 1) * TILE] = powers[i + 1][mine] / (
                factors[b] * (noise + EPSILON)
            )


def body(sizes, signal, replica, guard_cells, train_cells, scale_index, offsets):
    dims = plan(signal.shape, replica.shape, sizes)
    pieces, piece, gates, total, senders, tiles, panels, chunks, keeps = dims
    beams, pulses = signal.shape[0], signal.shape[1]
    rows = beams * pulses
    width = max(chunks * TILE + OFF_MAX, TILE + gates + sum(keeps))
    vmem = pl.BlockSpec(memory_space=pltpu.VMEM)
    placed = pl.BlockSpec(memory_space=pltpu.HBM)
    reach = len(keeps)
    planes = senders // sizes[1]
    operands = (offsets, guard_cells, train_cells, scale_index, signal, replica)
    gathered = pl.pallas_call(
        functools.partial(gather, sizes, dims),
        out_shape=(
            jax.ShapeDtypeStruct((senders, 2, piece), jnp.bfloat16),
            jax.ShapeDtypeStruct((chunks, 2 * rows, 2 * TILE), jnp.bfloat16),
            jax.ShapeDtypeStruct((beams, TILE, 3 * TILE), jnp.bfloat16),
            jax.ShapeDtypeStruct((beams, pulses, gates), jnp.float32),
            jax.ShapeDtypeStruct((beams, pulses, TILE), jnp.float32),
        ),
        in_specs=[placed] * 6,
        out_specs=(vmem,) * 5,
        scratch_shapes=[
            pltpu.VMEM((senders, 2, piece), jnp.bfloat16),
            pltpu.VMEM(signal.shape, jnp.bfloat16),
            pltpu.VMEM((beams, pulses, 2, TILE), jnp.bfloat16),
            pltpu.VMEM((width // TILE, 2 * rows, TILE), jnp.float32),
            pltpu.VMEM((2 * rows, width), jnp.float32),
        ]
        + [pltpu.SMEM((beams,), jnp.int32)] * 4
        + [
            pltpu.SemaphoreType.DMA((6,)),
            pltpu.SemaphoreType.DMA((1 + planes * (2 + sizes[0] - planes), sizes[1])),
            pltpu.SemaphoreType.DMA((senders,)),
            pltpu.SemaphoreType.DMA((reach + 1,)),
            pltpu.SemaphoreType.DMA((reach + 1,)),
            pltpu.SemaphoreType.REGULAR((max(sizes[0] - planes, 1),)),
        ]
        + [pltpu.VMEM((beams, pulses, 2, keep), jnp.bfloat16) for keep in keeps],
        compiler_params=pltpu.CompilerParams(
            collective_id=0, has_side_effects=True, vmem_limit_bytes=GRANT
        ),
        name="gather",
    )(*[pltpu.with_memory_space_constraint(v, pltpu.HBM) for v in operands])
    return pl.pallas_call(
        functools.partial(compute, sizes, dims),
        out_shape=(
            jax.ShapeDtypeStruct(signal.shape, jnp.bfloat16),
            jax.ShapeDtypeStruct((beams, pulses, gates), jnp.float32),
        ),
        in_specs=[vmem] * 5,
        out_specs=(vmem, vmem),
        scratch_shapes=[pltpu.VMEM((gates // TILE, 2 * rows, TILE), jnp.float32)],
        compiler_params=pltpu.CompilerParams(vmem_limit_bytes=GRANT),
        name="compute",
    )(*gathered)


def solution(mesh):
    placed = (
        P("beam", "pulse", None, "range"),
        P(None, ("beam", "pulse")),
        P("beam"),
        P("beam"),
        P("beam"),
        P("beam"),
    )
    sizes = (mesh.shape["beam"], mesh.shape["pulse"], mesh.shape["range"])
    return jax.shard_map(
        functools.partial(body, sizes),
        mesh=mesh,
        in_specs=placed,
        out_specs=(P("beam", "pulse", None, "range"), P("beam", "pulse", "range")),
        check_vma=False,
    )
```

```python
import functools

import jax
import jax.numpy as jnp
from jax import lax
from jax.experimental import pallas as pl
from jax.experimental.pallas import tpu as pltpu
from jax.sharding import PartitionSpec as P

TILE = 128
OFF_MAX = 128
EPSILON = 1e-06
GRANT = 24 << 20
MESH = pl.DeviceIdType.MESH


def plan(signal, replica, sizes):
    nb, npulse, nr = sizes
    pieces = nb * npulse
    piece = replica[1]
    gates = signal[3]
    total = gates * nr
    taps = min(piece * pieces, total)
    senders = -(-taps // (piece * npulse)) * npulse
    tiles = gates // TILE + 2
    panels = min(-(-piece * pieces // TILE) + 1, total // TILE)
    chunks = min(tiles + panels - 1, total // TILE + 1)
    beyond = (chunks - 1) * TILE - gates + OFF_MAX
    reach = min(-(-beyond // gates), nr - 1)
    keeps = [min(gates, beyond - s * gates) for s in range(reach)]
    return pieces, piece, gates, total, senders, tiles, panels, chunks, keeps


def gather(sizes, dims, *refs):
    pieces, piece, gates, total, senders, tiles, panels, chunks, keeps = dims
    nb, npulse, nr = sizes
    numbers, (sig, rep) = refs[:4], refs[4:6]
    hout, xa, weights, counts, factors = refs[6:11]
    hbuf, own, left, xf, yf = refs[11:16]
    offsets, guards, trains, scales = refs[16:20]
    here, hsend, hrecv, xsend, xrecv, ready = refs[20:26]
    right = refs[26:]
    beams, pulses = sig.shape[0], sig.shape[1]
    rows = beams * pulses
    bi, pi, ri = lax.axis_index("beam"), lax.axis_index("pulse"), lax.axis_index("range")
    me = bi * npulse + pi
    planes = senders // npulse
    reach = len(keeps)

    def say(semaphore, plane, pulse):
        pl.semaphore_signal(
            semaphore,
            inc=1,
            device_id={"beam": plane, "pulse": pulse},
            device_id_type=MESH,
        )

    barrier = pltpu.get_barrier_semaphore()

    @pl.when(bi < planes)
    def _():
        for j in range(1, npulse):
            say(barrier, bi, lax.rem(pi + j, npulse))

    for side in (-1, 1):

        @pl.when((bi < planes) & (bi + side >= 0) & (bi + side < planes))
        def _():
            for j in range(npulse):
                say(barrier, bi + side, lax.rem(pi + j, npulse))

    @pl.when(bi == planes - 1)
    def _():
        for q in range(planes, nb):
            for j in range(npulse):
                say(barrier, q, lax.rem(pi + j, npulse))

    for s in range(1, reach + 1):

        @pl.when(ri + s < nr)
        def _():
            pl.semaphore_signal(
                barrier, inc=1, device_id={"range": ri + s}, device_id_type=MESH
            )

    @pl.when(ri >= 1)
    def _():
        pl.semaphore_signal(
            barrier, inc=1, device_id={"range": ri - 1}, device_id_type=MESH
        )

    local = [pltpu.make_async_copy(sig, own, here.at[0])]
    for n, (number, kept) in enumerate(zip(numbers, (offsets, guards, trains, scales))):
        local.append(pltpu.make_async_copy(number, kept, here.at[n + 1]))
    for copy in local:
        copy.start()

    def head_copy(s):
        return pltpu.make_async_remote_copy(
            src_ref=sig.at[:, :, :, pl.ds(0, keeps[s - 1])],
            dst_ref=right[s - 1],
            send_sem=xsend.at[s],
            recv_sem=xrecv.at[s],
            device_id={"range": ri - s},
            device_id_type=MESH,
        )

    def tail_copy():
        return pltpu.make_async_remote_copy(
            src_ref=sig.at[:, :, :, pl.ds(gates - TILE, TILE)],
            dst_ref=left,
            send_sem=xsend.at[0],
            recv_sem=xrecv.at[0],
            device_id={"range": ri + 1},
            device_id_type=MESH,
        )

    def tap_copies(source, slot, way, plane):
        return [
            pltpu.make_async_remote_copy(
                src_ref=source,
                dst_ref=hbuf.at[slot],
                send_sem=hsend.at[way, j],
                recv_sem=hrecv.at[slot],
                device_id={"beam": plane, "pulse": lax.rem(pi + j, npulse)},
                device_id_type=MESH,
            )
            for j in range(1 if way == 0 else 0, npulse)
        ]

    def same_plane():
        return tap_copies(rep, pi * planes + bi, 0, bi)

    def down(b, source):
        return tap_copies(source, pi * planes + b, 1 + b, bi - 1)

    def up(b, source):
        return tap_copies(source, pi * planes + b, 1 + planes + b, bi + 1)

    def beyond(q):
        column = hbuf.at[pl.ds(pi * planes, planes)]
        return [
            pltpu.make_async_remote_copy(
                src_ref=column,
                dst_ref=column,
                send_sem=hsend.at[1 + planes + q, j],
                recv_sem=hrecv.at[pi * planes],
                device_id={"beam": q, "pulse": lax.rem(pi + j, npulse)},
                device_id_type=MESH,
            )
            for j in range(npulse)
        ]

    def arrived(slot, count=1):
        spot = hbuf.at[pl.ds(slot, count)]
        copy = pltpu.make_async_remote_copy(
            src_ref=spot,
            dst_ref=spot,
            send_sem=hsend.at[0, 0],
            recv_sem=hrecv.at[slot],
            device_id={"beam": bi},
            device_id_type=MESH,
        )
        copy.wait_recv()

    expect = jnp.minimum(ri, reach) + jnp.where(ri + 1 < nr, 1, 0)
    beside = jnp.where(bi >= 1, npulse, 0) + jnp.where(bi + 1 < planes, npulse, 0)
    expect += jnp.where(bi < planes, npulse - 1 + beside, npulse)
    pl.semaphore_wait(barrier, expect)

    for q in range(planes, nb):

        @pl.when(bi == q)
        def _():
            for j in range(npulse):
                say(ready.at[q - planes], planes - 1, lax.rem(pi + j, npulse))

    for b in range(planes):

        @pl.when(bi == b)
        def _():
            if b >= 1:
                for copy in down(b, rep):
                    copy.start()
            rest = same_plane()
            if b + 1 < planes:
                first, *others = up(b, rep)
                rest = [first] + rest + others
            for copy in rest:
                copy.start()

    for s in range(1, reach + 1):

        @pl.when(ri - s >= 0)
        def _():
            head_copy(s).start()

    @pl.when(ri + 1 < nr)
    def _():
        tail_copy().start()

    def own_taps():
        return pltpu.make_async_copy(rep, hbuf.at[pi * planes + bi], here.at[5])

    @pl.when(me < senders)
    def _():
        own_taps().start()

    def place(source, start, width):
        for b in range(beams):
            for p in range(pulses):
                at = 2 * (b * pulses + p)
                pair = source[b, p].astype(jnp.float32)
                for c in range(width // TILE):
                    xf[start // TILE + c, at : at + 2, :] = pair[:, c * TILE : (c + 1) * TILE]

    def clear(start, stop):
        for c in range(start // TILE, stop // TILE):
            xf[c] = jnp.zeros((2 * rows, TILE), jnp.float32)

    for copy in local:
        copy.wait()
    place(own, TILE, gates)
    tail = TILE + gates + sum(keeps)
    width = yf.shape[1]
    clear(tail, width)

    lane = lax.broadcasted_iota(jnp.int32, (TILE, 3 * TILE), 1)
    row = lax.broadcasted_iota(jnp.int32, (TILE, 3 * TILE), 0)
    apart = jnp.abs(lane - TILE - row)
    position = ri * gates + lax.broadcasted_iota(jnp.int32, (pulses, gates), 1)
    for b in range(beams):
        guard, train = guards[b], trains[b]
        inside = (apart > guard) & (apart <= guard + train)
        weights[b] = jnp.where(inside, 1.0, 0.0).astype(jnp.bfloat16)
        count = jnp.clip(position - guard, 0, train) + jnp.clip(
            total - 1 - position - guard, 0, train
        )
        counts[b] = count.astype(jnp.float32)
        level = jnp.full((pulses, TILE), scales[b], jnp.int32).astype(jnp.float32)
        factors[b] = jnp.exp2(level / 8.0)

    for b in reversed(range(planes)):

        @pl.when((bi < planes) & (bi != b) & (bi >= 1))
        def _():
            slot = pi * planes + b
            arrived(slot)

            @pl.when(bi < b)
            def _():
                for copy in down(b, hbuf.at[slot]):
                    copy.start()

            @pl.when((bi > b) & (bi + 1 < planes))
            def _():
                for copy in up(b, hbuf.at[slot]):
                    copy.start()

    @pl.when(bi == planes - 1)
    def _():
        own_taps().wait()
        for q in range(planes, nb):
            pl.semaphore_wait(ready.at[q - planes], npulse)
            for copy in beyond(q):
                copy.start()

    @pl.when(ri >= 1)
    def _():
        tail_copy().wait_recv()
        place(left, 0, TILE)

    @pl.when(ri == 0)
    def _():
        clear(0, TILE)

    at = TILE + gates
    for s in range(1, reach + 1):
        start, keep = at, keeps[s - 1]

        @pl.when(ri + s < nr)
        def _():
            head_copy(s).wait_recv()
            place(right[s - 1], start, keep)

        @pl.when(ri + s >= nr)
        def _():
            clear(start, start + keep)

        at += keep

    for b in range(beams):
        low = 2 * b * pulses
        real, imag = [
            pltpu.roll(
                jnp.concatenate(
                    [
                        xf[c, pl.ds(low + part, pulses, stride=2), :]
                        for c in range(width // TILE)
                    ],
                    axis=1,
                ),
                width - offsets[b],
                1,
            )
            for part in range(2)
        ]
        yf[b * pulses : (b + 1) * pulses, :] = real
        yf[rows + b * pulses : rows + (b + 1) * pulses, :] = imag
    for c in range(chunks):
        real = yf[:rows, c * TILE : (c + 1) * TILE]
        imag = yf[rows:, c * TILE : (c + 1) * TILE]
        first = jnp.concatenate([real, imag], axis=1)
        second = jnp.concatenate([imag, -real], axis=1)
        xa[c] = jnp.concatenate([first, second], axis=0).astype(jnp.bfloat16)

    @pl.when(bi < planes - 1)
    def _():
        own_taps().wait()

    for slot in range(senders):

        late = (bi == 0) & (slot % planes > 0)

        @pl.when((bi < planes) & ((pi != slot // planes) | late))
        def _():
            arrived(slot)

    for j in range(npulse):

        @pl.when(bi >= planes)
        def _():
            arrived(j * planes, planes)

    hout[...] = hbuf[...]

    @pl.when(bi < planes)
    def _():
        for copy in same_plane():
            copy.wait_send()

    for b in range(planes):

        @pl.when((bi < planes) & (bi <= b) & (bi >= 1))
        def _():
            for copy in down(b, rep):
                copy.wait_send()

        @pl.when((bi >= b) & (bi + 1 < planes))
        def _():
            for copy in up(b, rep):
                copy.wait_send()

    @pl.when(bi == planes - 1)
    def _():
        for q in range(planes, nb):
            for copy in beyond(q):
                copy.wait_send()

    for s in range(1, reach + 1):

        @pl.when(ri - s >= 0)
        def _():
            head_copy(s).wait_send()

    @pl.when(ri + 1 < nr)
    def _():
        tail_copy().wait_send()


def compute(sizes, dims, taps_ref, xa, weights, counts, factors, comp, ratio, xf):
    pieces, piece, gates, total, senders, tiles, panels, chunks, keeps = dims
    beams, pulses = comp.shape[0], comp.shape[1]
    rows = beams * pulses
    ri = lax.axis_index("range")

    across = tiles - 2

    per = TILE // piece if piece < TILE else 1
    spread = max(piece // TILE, 1)

    planes = senders // sizes[1]

    def taps_at(s):
        return taps_ref[(s % sizes[1]) * planes + s // sizes[1]].astype(jnp.float32)

    def taps_of(c):
        if piece >= TILE:
            return taps_at(c // spread)[
                :, (c % spread) * TILE : (c % spread + 1) * TILE
            ]
        parts = [taps_at(c * per + i) for i in range(per)]
        return jnp.concatenate(parts, axis=1)

    held = min(panels, (senders * piece) // TILE)
    lane = lax.broadcasted_iota(jnp.int32, (TILE, TILE), 1)
    row = lax.broadcasted_iota(jnp.int32, (TILE, TILE), 0)
    ahead = lane >= row

    def skewed(values):
        flat = jnp.broadcast_to(values, (TILE, TILE))
        return pltpu.roll(flat, 0, 1, stride=1, stride_axis=0)

    zero = jnp.zeros((TILE, TILE), jnp.float32)
    before = (zero, zero)
    sums = [None] * tiles
    for c in range(panels):
        if c < held:
            taps = taps_of(c)
            now = (skewed(taps[0:1]), skewed(taps[1:2]))
        else:
            now = (zero, zero)
        panel = jnp.concatenate(
            [jnp.where(ahead, n, b) for n, b in zip(now, before)], axis=1
        ).astype(jnp.bfloat16)
        before = now
        n = min(tiles, chunks - c)
        left_side = xa[c : c + n].reshape(n * 2 * rows, 2 * TILE)
        product = lax.dot_general(
            left_side, panel, (((1,), (1,)), ((), ())), preferred_element_type=jnp.float32
        )
        for i in range(n):
            part = product[i * 2 * rows : (i + 1) * 2 * rows]
            sums[i] = part if sums[i] is None else sums[i] + part

    powers = []
    for i in range(tiles):
        rounded = sums[i].astype(jnp.bfloat16).astype(jnp.float32)
        real, imag = rounded[:rows], rounded[rows:]
        power = real * real + imag * imag
        if i == 0:
            power = jnp.where(ri >= 1, power, 0.0)
        powers.append(power)
        if 1 <= i <= across:
            xf[i - 1, pl.ds(0, rows, stride=2), :] = real
            xf[i - 1, pl.ds(1, rows, stride=2), :] = imag
    for b in range(beams):
        for p in range(pulses):
            at = 2 * (b * pulses + p)
            for i in range(across):
                comp[b, p, :, i * TILE : (i + 1) * TILE] = xf[i, at : at + 2, :].astype(
                    jnp.bfloat16
                )

    split = []
    for power in powers:
        high = power.astype(jnp.bfloat16)
        rest = power - high.astype(jnp.float32)
        middle = rest.astype(jnp.bfloat16)
        low = (rest - middle.astype(jnp.float32)).astype(jnp.bfloat16)
        split.append([v.astype(jnp.float32) for v in (high, middle, low)])
    for b in range(beams):
        mine = slice(b * pulses, (b + 1) * pulses)
        side = jnp.concatenate(
            [
                jnp.concatenate([split[i + d][k][mine] for d in range(3)], axis=1)
                for i in range(across)
                for k in range(3)
            ],
            axis=0,
        ).astype(jnp.bfloat16)
        window = lax.dot_general(
            side, weights[b], (((1,), (1,)), ((), ())), preferred_element_type=jnp.float32
        )
        for i in range(across):
            base = 3 * i * pulses
            noise = (
                window[base : base + pulses]
                + window[base + pulses : base + 2 * pulses]
                + window[base + 2 * pulses : base + 3 * pulses]
            ) / counts[b, :, i * TILE : (i + 1) * TILE]
            ratio[b, :, i * TILE : (i + 1) * TILE] = powers[i + 1][mine] / (
                factors[b] * (noise + EPSILON)
            )


def body(sizes, signal, replica, guard_cells, train_cells, scale_index, offsets):
    dims = plan(signal.shape, replica.shape, sizes)
    pieces, piece, gates, total, senders, tiles, panels, chunks, keeps = dims
    beams, pulses = signal.shape[0], signal.shape[1]
    rows = beams * pulses
    width = max(chunks * TILE + OFF_MAX, TILE + gates + sum(keeps))
    vmem = pl.BlockSpec(memory_space=pltpu.VMEM)
    placed = pl.BlockSpec(memory_space=pltpu.HBM)
    reach = len(keeps)
    planes = senders // sizes[1]
    operands = (offsets, guard_cells, train_cells, scale_index, signal, replica)
    gathered = pl.pallas_call(
        functools.partial(gather, sizes, dims),
        out_shape=(
            jax.ShapeDtypeStruct((senders, 2, piece), jnp.bfloat16),
            jax.ShapeDtypeStruct((chunks, 2 * rows, 2 * TILE), jnp.bfloat16),
            jax.ShapeDtypeStruct((beams, TILE, 3 * TILE), jnp.bfloat16),
            jax.ShapeDtypeStruct((beams, pulses, gates), jnp.float32),
            jax.ShapeDtypeStruct((beams, pulses, TILE), jnp.float32),
        ),
        in_specs=[placed] * 6,
        out_specs=(vmem,) * 5,
        scratch_shapes=[
            pltpu.VMEM((senders, 2, piece), jnp.bfloat16),
            pltpu.VMEM(signal.shape, jnp.bfloat16),
            pltpu.VMEM((beams, pulses, 2, TILE), jnp.bfloat16),
            pltpu.VMEM((width // TILE, 2 * rows, TILE), jnp.float32),
            pltpu.VMEM((2 * rows, width), jnp.float32),
        ]
        + [pltpu.SMEM((beams,), jnp.int32)] * 4
        + [
            pltpu.SemaphoreType.DMA((6,)),
            pltpu.SemaphoreType.DMA((1 + 2 * planes + sizes[0], sizes[1])),
            pltpu.SemaphoreType.DMA((senders,)),
            pltpu.SemaphoreType.DMA((reach + 1,)),
            pltpu.SemaphoreType.DMA((reach + 1,)),
            pltpu.SemaphoreType.REGULAR((max(sizes[0] - planes, 1),)),
        ]
        + [pltpu.VMEM((beams, pulses, 2, keep), jnp.bfloat16) for keep in keeps],
        compiler_params=pltpu.CompilerParams(
            collective_id=0, has_side_effects=True, vmem_limit_bytes=GRANT
        ),
        name="gather",
    )(*[pltpu.with_memory_space_constraint(v, pltpu.HBM) for v in operands])
    return pl.pallas_call(
        functools.partial(compute, sizes, dims),
        out_shape=(
            jax.ShapeDtypeStruct(signal.shape, jnp.bfloat16),
            jax.ShapeDtypeStruct((beams, pulses, gates), jnp.float32),
        ),
        in_specs=[vmem] * 5,
        out_specs=(vmem, vmem),
        scratch_shapes=[pltpu.VMEM((gates // TILE, 2 * rows, TILE), jnp.float32)],
        compiler_params=pltpu.CompilerParams(vmem_limit_bytes=GRANT),
        name="compute",
    )(*gathered)


def solution(mesh):
    placed = (
        P("beam", "pulse", None, "range"),
        P(None, ("beam", "pulse")),
        P("beam"),
        P("beam"),
        P("beam"),
        P("beam"),
    )
    sizes = (mesh.shape["beam"], mesh.shape["pulse"], mesh.shape["range"])
    return jax.shard_map(
        functools.partial(body, sizes),
        mesh=mesh,
        in_specs=placed,
        out_specs=(P("beam", "pulse", None, "range"), P("beam", "pulse", "range")),
        check_vma=False,
    )
```

```python
import functools

import jax
import jax.numpy as jnp
from jax import lax
from jax.experimental import pallas as pl
from jax.experimental.pallas import tpu as pltpu
from jax.sharding import PartitionSpec as P

TILE = 128
OFF_MAX = 128
EPSILON = 1e-06
GRANT = 24 << 20
MESH = pl.DeviceIdType.MESH


def plan(signal, replica, sizes):
    nb, npulse, nr = sizes
    pieces = nb * npulse
    piece = replica[1]
    gates = signal[3]
    total = gates * nr
    taps = min(piece * pieces, total)
    senders = -(-taps // (piece * npulse)) * npulse
    tiles = gates // TILE + 2
    panels = min(-(-piece * pieces // TILE) + 1, total // TILE)
    chunks = min(tiles + panels - 1, total // TILE + 1)
    beyond = (chunks - 1) * TILE - gates + OFF_MAX
    reach = min(-(-beyond // gates), nr - 1)
    keeps = [min(gates, beyond - s * gates) for s in range(reach)]
    return pieces, piece, gates, total, senders, tiles, panels, chunks, keeps


def gather(sizes, dims, *refs):
    pieces, piece, gates, total, senders, tiles, panels, chunks, keeps = dims
    nb, npulse, nr = sizes
    numbers, (sig, rep) = refs[:4], refs[4:6]
    hout, xa, weights, counts, factors = refs[6:11]
    hbuf, own, left, xf, yf = refs[11:16]
    offsets, guards, trains, scales = refs[16:20]
    here, hsend, hrecv, xsend, xrecv, ready = refs[20:26]
    right = refs[26:]
    beams, pulses = sig.shape[0], sig.shape[1]
    rows = beams * pulses
    bi, pi, ri = lax.axis_index("beam"), lax.axis_index("pulse"), lax.axis_index("range")
    me = bi * npulse + pi
    planes = senders // npulse
    reach = len(keeps)

    def say(semaphore, plane, pulse):
        pl.semaphore_signal(
            semaphore,
            inc=1,
            device_id={"beam": plane, "pulse": pulse},
            device_id_type=MESH,
        )

    barrier = pltpu.get_barrier_semaphore()

    @pl.when(bi < planes)
    def _():
        for j in range(1, npulse):
            say(barrier, bi, lax.rem(pi + j, npulse))

    for side in (-1, 1):

        @pl.when((bi < planes) & (bi + side >= 0) & (bi + side < planes))
        def _():
            for j in range(npulse):
                say(barrier, bi + side, lax.rem(pi + j, npulse))

    @pl.when(bi == planes - 1)
    def _():
        for q in range(planes, nb):
            for j in range(npulse):
                say(barrier, q, lax.rem(pi + j, npulse))

    for s in range(1, reach + 1):

        @pl.when(ri + s < nr)
        def _():
            pl.semaphore_signal(
                barrier, inc=1, device_id={"range": ri + s}, device_id_type=MESH
            )

    @pl.when(ri >= 1)
    def _():
        pl.semaphore_signal(
            barrier, inc=1, device_id={"range": ri - 1}, device_id_type=MESH
        )

    local = [pltpu.make_async_copy(sig, own, here.at[0])]
    for n, (number, kept) in enumerate(zip(numbers, (offsets, guards, trains, scales))):
        local.append(pltpu.make_async_copy(number, kept, here.at[n + 1]))
    for copy in local:
        copy.start()

    def head_copy(s):
        return pltpu.make_async_remote_copy(
            src_ref=sig.at[:, :, :, pl.ds(0, keeps[s - 1])],
            dst_ref=right[s - 1],
            send_sem=xsend.at[s],
            recv_sem=xrecv.at[s],
            device_id={"range": ri - s},
            device_id_type=MESH,
        )

    def tail_copy():
        return pltpu.make_async_remote_copy(
            src_ref=sig.at[:, :, :, pl.ds(gates - TILE, TILE)],
            dst_ref=left,
            send_sem=xsend.at[0],
            recv_sem=xrecv.at[0],
            device_id={"range": ri + 1},
            device_id_type=MESH,
        )

    def tap_copies(source, slot, way, plane):
        return [
            pltpu.make_async_remote_copy(
                src_ref=source,
                dst_ref=hbuf.at[slot],
                send_sem=hsend.at[way, j],
                recv_sem=hrecv.at[slot],
                device_id={"beam": plane, "pulse": j},
                device_id_type=MESH,
            )
            for j in range(npulse)
        ]

    def same_plane():
        return tap_copies(rep, pi * planes + bi, 0, bi)

    def down(b, source):
        return tap_copies(source, pi * planes + b, 1 + b, bi - 1)

    def up(b, source):
        return tap_copies(source, pi * planes + b, 1 + planes + b, bi + 1)

    def beyond(q):
        column = hbuf.at[pl.ds(pi * planes, planes)]
        return [
            pltpu.make_async_remote_copy(
                src_ref=column,
                dst_ref=column,
                send_sem=hsend.at[1 + planes + q, j],
                recv_sem=hrecv.at[pi * planes],
                device_id={"beam": q, "pulse": lax.rem(pi + j, npulse)},
                device_id_type=MESH,
            )
            for j in range(npulse)
        ]

    def arrived(slot, count=1):
        spot = hbuf.at[pl.ds(slot, count)]
        copy = pltpu.make_async_remote_copy(
            src_ref=spot,
            dst_ref=spot,
            send_sem=hsend.at[0, 0],
            recv_sem=hrecv.at[slot],
            device_id={"beam": bi},
            device_id_type=MESH,
        )
        copy.wait_recv()

    expect = jnp.minimum(ri, reach) + jnp.where(ri + 1 < nr, 1, 0)
    beside = jnp.where(bi >= 1, npulse, 0) + jnp.where(bi + 1 < planes, npulse, 0)
    expect += jnp.where(bi < planes, npulse - 1 + beside, npulse)
    pl.semaphore_wait(barrier, expect)

    for q in range(planes, nb):

        @pl.when(bi == q)
        def _():
            for j in range(npulse):
                say(ready.at[q - planes], planes - 1, lax.rem(pi + j, npulse))

    for b in range(planes):

        @pl.when(bi == b)
        def _():
            if b >= 1:
                for copy in down(b, rep):
                    copy.start()
            for j, copy in enumerate(same_plane()):
                pl.when(pi != j)(copy.start)
            if b + 1 < planes:
                for copy in up(b, rep):
                    copy.start()

    for s in range(1, reach + 1):

        @pl.when(ri - s >= 0)
        def _():
            head_copy(s).start()

    @pl.when(ri + 1 < nr)
    def _():
        tail_copy().start()

    def own_taps():
        return pltpu.make_async_copy(rep, hbuf.at[pi * planes + bi], here.at[5])

    @pl.when(me < senders)
    def _():
        own_taps().start()

    def place(source, start, width):
        for b in range(beams):
            for p in range(pulses):
                at = 2 * (b * pulses + p)
                pair = source[b, p].astype(jnp.float32)
                for c in range(width // TILE):
                    xf[start // TILE + c, at : at + 2, :] = pair[:, c * TILE : (c + 1) * TILE]

    def clear(start, stop):
        for c in range(start // TILE, stop // TILE):
            xf[c] = jnp.zeros((2 * rows, TILE), jnp.float32)

    for copy in local:
        copy.wait()
    place(own, TILE, gates)
    tail = TILE + gates + sum(keeps)
    width = yf.shape[1]
    clear(tail, width)

    lane = lax.broadcasted_iota(jnp.int32, (TILE, 3 * TILE), 1)
    row = lax.broadcasted_iota(jnp.int32, (TILE, 3 * TILE), 0)
    apart = jnp.abs(lane - TILE - row)
    position = ri * gates + lax.broadcasted_iota(jnp.int32, (pulses, gates), 1)
    for b in range(beams):
        guard, train = guards[b], trains[b]
        inside = (apart > guard) & (apart <= guard + train)
        weights[b] = jnp.where(inside, 1.0, 0.0).astype(jnp.bfloat16)
        count = jnp.clip(position - guard, 0, train) + jnp.clip(
            total - 1 - position - guard, 0, train
        )
        counts[b] = count.astype(jnp.float32)
        level = jnp.full((pulses, TILE), scales[b], jnp.int32).astype(jnp.float32)
        factors[b] = jnp.exp2(level / 8.0)

    for b in reversed(range(planes)):

        @pl.when((bi < planes) & (bi != b) & (bi >= 1))
        def _():
            slot = pi * planes + b
            arrived(slot)

            @pl.when(bi < b)
            def _():
                for copy in down(b, hbuf.at[slot]):
                    copy.start()

            @pl.when((bi > b) & (bi + 1 < planes))
            def _():
                for copy in up(b, hbuf.at[slot]):
                    copy.start()

    @pl.when(bi == planes - 1)
    def _():
        own_taps().wait()
        for q in range(planes, nb):
            pl.semaphore_wait(ready.at[q - planes], npulse)
            for copy in beyond(q):
                copy.start()

    @pl.when(ri >= 1)
    def _():
        tail_copy().wait_recv()
        place(left, 0, TILE)

    @pl.when(ri == 0)
    def _():
        clear(0, TILE)

    at = TILE + gates
    for s in range(1, reach + 1):
        start, keep = at, keeps[s - 1]

        @pl.when(ri + s < nr)
        def _():
            head_copy(s).wait_recv()
            place(right[s - 1], start, keep)

        @pl.when(ri + s >= nr)
        def _():
            clear(start, start + keep)

        at += keep

    for b in range(beams):
        low = 2 * b * pulses
        real, imag = [
            pltpu.roll(
                jnp.concatenate(
                    [
                        xf[c, pl.ds(low + part, pulses, stride=2), :]
                        for c in range(width // TILE)
                    ],
                    axis=1,
                ),
                width - offsets[b],
                1,
            )
            for part in range(2)
        ]
        yf[b * pulses : (b + 1) * pulses, :] = real
        yf[rows + b * pulses : rows + (b + 1) * pulses, :] = imag
    for c in range(chunks):
        real = yf[:rows, c * TILE : (c + 1) * TILE]
        imag = yf[rows:, c * TILE : (c + 1) * TILE]
        first = jnp.concatenate([real, imag], axis=1)
        second = jnp.concatenate([imag, -real], axis=1)
        xa[c] = jnp.concatenate([first, second], axis=0).astype(jnp.bfloat16)

    @pl.when(bi < planes - 1)
    def _():
        own_taps().wait()

    for slot in range(senders):

        late = (bi == 0) & (slot % planes > 0)

        @pl.when((bi < planes) & ((pi != slot // planes) | late))
        def _():
            arrived(slot)

    for j in range(npulse):

        @pl.when(bi >= planes)
        def _():
            arrived(j * planes, planes)

    hout[...] = hbuf[...]

    @pl.when(bi < planes)
    def _():
        for j, copy in enumerate(same_plane()):
            pl.when(pi != j)(copy.wait_send)

    for b in range(planes):

        @pl.when((bi < planes) & (bi <= b) & (bi >= 1))
        def _():
            for copy in down(b, rep):
                copy.wait_send()

        @pl.when((bi >= b) & (bi + 1 < planes))
        def _():
            for copy in up(b, rep):
                copy.wait_send()

    @pl.when(bi == planes - 1)
    def _():
        for q in range(planes, nb):
            for copy in beyond(q):
                copy.wait_send()

    for s in range(1, reach + 1):

        @pl.when(ri - s >= 0)
        def _():
            head_copy(s).wait_send()

    @pl.when(ri + 1 < nr)
    def _():
        tail_copy().wait_send()


def compute(sizes, dims, taps_ref, xa, weights, counts, factors, comp, ratio, xf):
    pieces, piece, gates, total, senders, tiles, panels, chunks, keeps = dims
    beams, pulses = comp.shape[0], comp.shape[1]
    rows = beams * pulses
    ri = lax.axis_index("range")

    across = tiles - 2

    per = TILE // piece if piece < TILE else 1
    spread = max(piece // TILE, 1)

    planes = senders // sizes[1]

    def taps_at(s):
        return taps_ref[(s % sizes[1]) * planes + s // sizes[1]].astype(jnp.float32)

    def taps_of(c):
        if piece >= TILE:
            return taps_at(c // spread)[
                :, (c % spread) * TILE : (c % spread + 1) * TILE
            ]
        parts = [taps_at(c * per + i) for i in range(per)]
        return jnp.concatenate(parts, axis=1)

    held = min(panels, (senders * piece) // TILE)
    lane = lax.broadcasted_iota(jnp.int32, (TILE, TILE), 1)
    row = lax.broadcasted_iota(jnp.int32, (TILE, TILE), 0)
    ahead = lane >= row

    def skewed(values):
        flat = jnp.broadcast_to(values, (TILE, TILE))
        return pltpu.roll(flat, 0, 1, stride=1, stride_axis=0)

    zero = jnp.zeros((TILE, TILE), jnp.float32)
    before = (zero, zero)
    sums = [None] * tiles
    for c in range(panels):
        if c < held:
            taps = taps_of(c)
            now = (skewed(taps[0:1]), skewed(taps[1:2]))
        else:
            now = (zero, zero)
        panel = jnp.concatenate(
            [jnp.where(ahead, n, b) for n, b in zip(now, before)], axis=1
        ).astype(jnp.bfloat16)
        before = now
        n = min(tiles, chunks - c)
        left_side = xa[c : c + n].reshape(n * 2 * rows, 2 * TILE)
        product = lax.dot_general(
            left_side, panel, (((1,), (1,)), ((), ())), preferred_element_type=jnp.float32
        )
        for i in range(n):
            part = product[i * 2 * rows : (i + 1) * 2 * rows]
            sums[i] = part if sums[i] is None else sums[i] + part

    powers = []
    for i in range(tiles):
        rounded = sums[i].astype(jnp.bfloat16).astype(jnp.float32)
        real, imag = rounded[:rows], rounded[rows:]
        power = real * real + imag * imag
        if i == 0:
            power = jnp.where(ri >= 1, power, 0.0)
        powers.append(power)
        if 1 <= i <= across:
            xf[i - 1, pl.ds(0, rows, stride=2), :] = real
            xf[i - 1, pl.ds(1, rows, stride=2), :] = imag
    for b in range(beams):
        for p in range(pulses):
            at = 2 * (b * pulses + p)
            for i in range(across):
                comp[b, p, :, i * TILE : (i + 1) * TILE] = xf[i, at : at + 2, :].astype(
                    jnp.bfloat16
                )

    split = []
    for power in powers:
        high = power.astype(jnp.bfloat16)
        rest = power - high.astype(jnp.float32)
        middle = rest.astype(jnp.bfloat16)
        low = (rest - middle.astype(jnp.float32)).astype(jnp.bfloat16)
        split.append([v.astype(jnp.float32) for v in (high, middle, low)])
    for b in range(beams):
        mine = slice(b * pulses, (b + 1) * pulses)
        side = jnp.concatenate(
            [
                jnp.concatenate([split[i + d][k][mine] for d in range(3)], axis=1)
                for i in range(across)
                for k in range(3)
            ],
            axis=0,
        ).astype(jnp.bfloat16)
        window = lax.dot_general(
            side, weights[b], (((1,), (1,)), ((), ())), preferred_element_type=jnp.float32
        )
        for i in range(across):
            base = 3 * i * pulses
            noise = (
                window[base : base + pulses]
                + window[base + pulses : base + 2 * pulses]
                + window[base + 2 * pulses : base + 3 * pulses]
            ) / counts[b, :, i * TILE : (i + 1) * TILE]
            ratio[b, :, i * TILE : (i + 1) * TILE] = powers[i + 1][mine] / (
                factors[b] * (noise + EPSILON)
            )


def body(sizes, signal, replica, guard_cells, train_cells, scale_index, offsets):
    dims = plan(signal.shape, replica.shape, sizes)
    pieces, piece, gates, total, senders, tiles, panels, chunks, keeps = dims
    beams, pulses = signal.shape[0], signal.shape[1]
    rows = beams * pulses
    width = max(chunks * TILE + OFF_MAX, TILE + gates + sum(keeps))
    vmem = pl.BlockSpec(memory_space=pltpu.VMEM)
    placed = pl.BlockSpec(memory_space=pltpu.HBM)
    reach = len(keeps)
    planes = senders // sizes[1]
    operands = (offsets, guard_cells, train_cells, scale_index, signal, replica)
    gathered = pl.pallas_call(
        functools.partial(gather, sizes, dims),
        out_shape=(
            jax.ShapeDtypeStruct((senders, 2, piece), jnp.bfloat16),
            jax.ShapeDtypeStruct((chunks, 2 * rows, 2 * TILE), jnp.bfloat16),
            jax.ShapeDtypeStruct((beams, TILE, 3 * TILE), jnp.bfloat16),
            jax.ShapeDtypeStruct((beams, pulses, gates), jnp.float32),
            jax.ShapeDtypeStruct((beams, pulses, TILE), jnp.float32),
        ),
        in_specs=[placed] * 6,
        out_specs=(vmem,) * 5,
        scratch_shapes=[
            pltpu.VMEM((senders, 2, piece), jnp.bfloat16),
            pltpu.VMEM(signal.shape, jnp.bfloat16),
            pltpu.VMEM((beams, pulses, 2, TILE), jnp.bfloat16),
            pltpu.VMEM((width // TILE, 2 * rows, TILE), jnp.float32),
            pltpu.VMEM((2 * rows, width), jnp.float32),
        ]
        + [pltpu.SMEM((beams,), jnp.int32)] * 4
        + [
            pltpu.SemaphoreType.DMA((6,)),
            pltpu.SemaphoreType.DMA((1 + 2 * planes + sizes[0], sizes[1])),
            pltpu.SemaphoreType.DMA((senders,)),
            pltpu.SemaphoreType.DMA((reach + 1,)),
            pltpu.SemaphoreType.DMA((reach + 1,)),
            pltpu.SemaphoreType.REGULAR((max(sizes[0] - planes, 1),)),
        ]
        + [pltpu.VMEM((beams, pulses, 2, keep), jnp.bfloat16) for keep in keeps],
        compiler_params=pltpu.CompilerParams(
            collective_id=0, has_side_effects=True, vmem_limit_bytes=GRANT
        ),
        name="gather",
    )(*[pltpu.with_memory_space_constraint(v, pltpu.HBM) for v in operands])
    return pl.pallas_call(
        functools.partial(compute, sizes, dims),
        out_shape=(
            jax.ShapeDtypeStruct(signal.shape, jnp.bfloat16),
            jax.ShapeDtypeStruct((beams, pulses, gates), jnp.float32),
        ),
        in_specs=[vmem] * 5,
        out_specs=(vmem, vmem),
        scratch_shapes=[pltpu.VMEM((gates // TILE, 2 * rows, TILE), jnp.float32)],
        compiler_params=pltpu.CompilerParams(vmem_limit_bytes=GRANT),
        name="compute",
    )(*gathered)


def solution(mesh):
    placed = (
        P("beam", "pulse", None, "range"),
        P(None, ("beam", "pulse")),
        P("beam"),
        P("beam"),
        P("beam"),
        P("beam"),
    )
    sizes = (mesh.shape["beam"], mesh.shape["pulse"], mesh.shape["range"])
    return jax.shard_map(
        functools.partial(body, sizes),
        mesh=mesh,
        in_specs=placed,
        out_specs=(P("beam", "pulse", None, "range"), P("beam", "pulse", "range")),
        check_vma=False,
    )
```

```python
import functools

import jax
import jax.numpy as jnp
from jax import lax
from jax.experimental import pallas as pl
from jax.experimental.pallas import tpu as pltpu
from jax.sharding import PartitionSpec as P

TILE = 128
OFF_MAX = 128
EPSILON = 1e-06
GRANT = 24 << 20
MESH = pl.DeviceIdType.MESH


def plan(signal, replica, sizes):
    nb, npulse, nr = sizes
    pieces = nb * npulse
    piece = replica[1]
    gates = signal[3]
    total = gates * nr
    taps = min(piece * pieces, total)
    senders = -(-taps // (piece * npulse)) * npulse
    tiles = gates // TILE + 2
    panels = min(-(-piece * pieces // TILE) + 1, total // TILE)
    chunks = min(tiles + panels - 1, total // TILE + 1)
    beyond = (chunks - 1) * TILE - gates + OFF_MAX
    reach = min(-(-beyond // gates), nr - 1)
    keeps = [min(gates, beyond - s * gates) for s in range(reach)]
    return pieces, piece, gates, total, senders, tiles, panels, chunks, keeps


def gather(sizes, dims, *refs):
    pieces, piece, gates, total, senders, tiles, panels, chunks, keeps = dims
    nb, npulse, nr = sizes
    numbers, (sig, rep) = refs[:4], refs[4:6]
    hout, xa, weights, counts, factors = refs[6:11]
    hbuf, own, left, xf, yf = refs[11:16]
    offsets, guards, trains, scales = refs[16:20]
    here, hsend, hrecv, xsend, xrecv, ready = refs[20:26]
    right = refs[26:]
    beams, pulses = sig.shape[0], sig.shape[1]
    rows = beams * pulses
    bi, pi, ri = lax.axis_index("beam"), lax.axis_index("pulse"), lax.axis_index("range")
    me = bi * npulse + pi
    planes = senders // npulse
    reach = len(keeps)

    def say(semaphore, plane, pulse):
        pl.semaphore_signal(
            semaphore,
            inc=1,
            device_id={"beam": plane, "pulse": pulse},
            device_id_type=MESH,
        )

    barrier = pltpu.get_barrier_semaphore()

    @pl.when(bi < planes)
    def _():
        for j in range(1, npulse):
            say(barrier, bi, lax.rem(pi + j, npulse))

    @pl.when(bi + 1 < planes)
    def _():
        for j in range(npulse):
            say(barrier, bi + 1, lax.rem(pi + j, npulse))

    @pl.when(bi == planes - 1)
    def _():
        for q in range(planes, nb):
            for j in range(npulse):
                say(barrier, q, lax.rem(pi + j, npulse))

    for s in range(1, reach + 1):

        @pl.when(ri + s < nr)
        def _():
            pl.semaphore_signal(
                barrier, inc=1, device_id={"range": ri + s}, device_id_type=MESH
            )

    @pl.when(ri >= 1)
    def _():
        pl.semaphore_signal(
            barrier, inc=1, device_id={"range": ri - 1}, device_id_type=MESH
        )

    local = [pltpu.make_async_copy(sig, own, here.at[0])]
    for n, (number, kept) in enumerate(zip(numbers, (offsets, guards, trains, scales))):
        local.append(pltpu.make_async_copy(number, kept, here.at[n + 1]))
    for copy in local:
        copy.start()

    def head_copy(s):
        return pltpu.make_async_remote_copy(
            src_ref=sig.at[:, :, :, pl.ds(0, keeps[s - 1])],
            dst_ref=right[s - 1],
            send_sem=xsend.at[s],
            recv_sem=xrecv.at[s],
            device_id={"range": ri - s},
            device_id_type=MESH,
        )

    def tail_copy():
        return pltpu.make_async_remote_copy(
            src_ref=sig.at[:, :, :, pl.ds(gates - TILE, TILE)],
            dst_ref=left,
            send_sem=xsend.at[0],
            recv_sem=xrecv.at[0],
            device_id={"range": ri + 1},
            device_id_type=MESH,
        )

    def tap_copies(source, slot, way, plane):
        return [
            pltpu.make_async_remote_copy(
                src_ref=source,
                dst_ref=hbuf.at[slot],
                send_sem=hsend.at[way, j],
                recv_sem=hrecv.at[slot],
                device_id={"beam": plane, "pulse": j},
                device_id_type=MESH,
            )
            for j in range(npulse)
        ]

    def same_plane():
        return tap_copies(rep, pi * planes + bi, 0, bi)

    def down(b, source):
        return tap_copies(source, pi * planes + b, 1 + b, bi - 1)

    def up(b, source):
        return tap_copies(source, pi * planes + b, 1 + planes + b, bi + 1)

    def beyond(q):
        column = hbuf.at[pl.ds(pi * planes, planes)]
        return [
            pltpu.make_async_remote_copy(
                src_ref=column,
                dst_ref=column,
                send_sem=hsend.at[1 + planes + q, j],
                recv_sem=hrecv.at[pi * planes],
                device_id={"beam": q, "pulse": lax.rem(pi + j, npulse)},
                device_id_type=MESH,
            )
            for j in range(npulse)
        ]

    def arrived(slot, count=1):
        spot = hbuf.at[pl.ds(slot, count)]
        copy = pltpu.make_async_remote_copy(
            src_ref=spot,
            dst_ref=spot,
            send_sem=hsend.at[0, 0],
            recv_sem=hrecv.at[slot],
            device_id={"beam": bi},
            device_id_type=MESH,
        )
        copy.wait_recv()

    expect = jnp.minimum(ri, reach) + jnp.where(ri + 1 < nr, 1, 0)
    beside = jnp.where(bi >= 1, npulse, 0)
    expect += jnp.where(bi < planes, npulse - 1 + beside, npulse)
    pl.semaphore_wait(barrier, expect)
    above = ready.at[nb - planes]

    @pl.when((bi < planes) & (bi >= 1))
    def _():
        for j in range(npulse):
            say(above, bi - 1, lax.rem(pi + j, npulse))

    for q in range(planes, nb):

        @pl.when(bi == q)
        def _():
            for j in range(npulse):
                say(ready.at[q - planes], planes - 1, lax.rem(pi + j, npulse))

    for b in range(planes):

        @pl.when(bi == b)
        def _():
            if b >= 1:
                for copy in down(b, rep):
                    copy.start()
            for j, copy in enumerate(same_plane()):
                pl.when(pi != j)(copy.start)

    for s in range(1, reach + 1):

        @pl.when(ri - s >= 0)
        def _():
            head_copy(s).start()

    @pl.when(ri + 1 < nr)
    def _():
        tail_copy().start()

    def own_taps():
        return pltpu.make_async_copy(rep, hbuf.at[pi * planes + bi], here.at[5])

    @pl.when(me < senders)
    def _():
        own_taps().start()

    def place(source, start, width):
        for b in range(beams):
            for p in range(pulses):
                at = 2 * (b * pulses + p)
                pair = source[b, p].astype(jnp.float32)
                for c in range(width // TILE):
                    xf[start // TILE + c, at : at + 2, :] = pair[:, c * TILE : (c + 1) * TILE]

    def clear(start, stop):
        for c in range(start // TILE, stop // TILE):
            xf[c] = jnp.zeros((2 * rows, TILE), jnp.float32)

    for copy in local:
        copy.wait()
    place(own, TILE, gates)
    tail = TILE + gates + sum(keeps)
    width = yf.shape[1]
    clear(tail, width)

    lane = lax.broadcasted_iota(jnp.int32, (TILE, 3 * TILE), 1)
    row = lax.broadcasted_iota(jnp.int32, (TILE, 3 * TILE), 0)
    apart = jnp.abs(lane - TILE - row)
    position = ri * gates + lax.broadcasted_iota(jnp.int32, (pulses, gates), 1)
    for b in range(beams):
        guard, train = guards[b], trains[b]
        inside = (apart > guard) & (apart <= guard + train)
        weights[b] = jnp.where(inside, 1.0, 0.0).astype(jnp.bfloat16)
        count = jnp.clip(position - guard, 0, train) + jnp.clip(
            total - 1 - position - guard, 0, train
        )
        counts[b] = count.astype(jnp.float32)
        level = jnp.full((pulses, TILE), scales[b], jnp.int32).astype(jnp.float32)
        factors[b] = jnp.exp2(level / 8.0)

    @pl.when(bi + 1 < planes)
    def _():
        pl.semaphore_wait(above, npulse)
        for b in range(planes - 1):

            @pl.when(bi == b)
            def _():
                for copy in up(b, rep):
                    copy.start()

    for b in reversed(range(planes)):

        @pl.when((bi < planes) & (bi != b) & (bi >= 1))
        def _():
            slot = pi * planes + b
            arrived(slot)

            @pl.when(bi < b)
            def _():
                for copy in down(b, hbuf.at[slot]):
                    copy.start()

            @pl.when((bi > b) & (bi + 1 < planes))
            def _():
                for copy in up(b, hbuf.at[slot]):
                    copy.start()

    @pl.when(bi == planes - 1)
    def _():
        own_taps().wait()
        for q in range(planes, nb):
            pl.semaphore_wait(ready.at[q - planes], npulse)
            for copy in beyond(q):
                copy.start()

    @pl.when(ri >= 1)
    def _():
        tail_copy().wait_recv()
        place(left, 0, TILE)

    @pl.when(ri == 0)
    def _():
        clear(0, TILE)

    at = TILE + gates
    for s in range(1, reach + 1):
        start, keep = at, keeps[s - 1]

        @pl.when(ri + s < nr)
        def _():
            head_copy(s).wait_recv()
            place(right[s - 1], start, keep)

        @pl.when(ri + s >= nr)
        def _():
            clear(start, start + keep)

        at += keep

    for b in range(beams):
        low = 2 * b * pulses
        real, imag = [
            pltpu.roll(
                jnp.concatenate(
                    [
                        xf[c, pl.ds(low + part, pulses, stride=2), :]
                        for c in range(width // TILE)
                    ],
                    axis=1,
                ),
                width - offsets[b],
                1,
            )
            for part in range(2)
        ]
        yf[b * pulses : (b + 1) * pulses, :] = real
        yf[rows + b * pulses : rows + (b + 1) * pulses, :] = imag
    for c in range(chunks):
        real = yf[:rows, c * TILE : (c + 1) * TILE]
        imag = yf[rows:, c * TILE : (c + 1) * TILE]
        first = jnp.concatenate([real, imag], axis=1)
        second = jnp.concatenate([imag, -real], axis=1)
        xa[c] = jnp.concatenate([first, second], axis=0).astype(jnp.bfloat16)

    @pl.when(bi < planes - 1)
    def _():
        own_taps().wait()

    for slot in range(senders):

        late = (bi == 0) & (slot % planes > 0)

        @pl.when((bi < planes) & ((pi != slot // planes) | late))
        def _():
            arrived(slot)

    for j in range(npulse):

        @pl.when(bi >= planes)
        def _():
            arrived(j * planes, planes)

    hout[...] = hbuf[...]

    @pl.when(bi < planes)
    def _():
        for j, copy in enumerate(same_plane()):
            pl.when(pi != j)(copy.wait_send)

    for b in range(planes):

        @pl.when((bi < planes) & (bi <= b) & (bi >= 1))
        def _():
            for copy in down(b, rep):
                copy.wait_send()

        @pl.when((bi >= b) & (bi + 1 < planes))
        def _():
            for copy in up(b, rep):
                copy.wait_send()

    @pl.when(bi == planes - 1)
    def _():
        for q in range(planes, nb):
            for copy in beyond(q):
                copy.wait_send()

    for s in range(1, reach + 1):

        @pl.when(ri - s >= 0)
        def _():
            head_copy(s).wait_send()

    @pl.when(ri + 1 < nr)
    def _():
        tail_copy().wait_send()


def compute(sizes, dims, taps_ref, xa, weights, counts, factors, comp, ratio, xf):
    pieces, piece, gates, total, senders, tiles, panels, chunks, keeps = dims
    beams, pulses = comp.shape[0], comp.shape[1]
    rows = beams * pulses
    ri = lax.axis_index("range")

    across = tiles - 2

    per = TILE // piece if piece < TILE else 1
    spread = max(piece // TILE, 1)

    planes = senders // sizes[1]

    def taps_at(s):
        return taps_ref[(s % sizes[1]) * planes + s // sizes[1]].astype(jnp.float32)

    def taps_of(c):
        if piece >= TILE:
            return taps_at(c // spread)[
                :, (c % spread) * TILE : (c % spread + 1) * TILE
            ]
        parts = [taps_at(c * per + i) for i in range(per)]
        return jnp.concatenate(parts, axis=1)

    held = min(panels, (senders * piece) // TILE)
    lane = lax.broadcasted_iota(jnp.int32, (TILE, TILE), 1)
    row = lax.broadcasted_iota(jnp.int32, (TILE, TILE), 0)
    ahead = lane >= row

    def skewed(values):
        flat = jnp.broadcast_to(values, (TILE, TILE))
        return pltpu.roll(flat, 0, 1, stride=1, stride_axis=0)

    zero = jnp.zeros((TILE, TILE), jnp.float32)
    before = (zero, zero)
    sums = [None] * tiles
    for c in range(panels):
        if c < held:
            taps = taps_of(c)
            now = (skewed(taps[0:1]), skewed(taps[1:2]))
        else:
            now = (zero, zero)
        panel = jnp.concatenate(
            [jnp.where(ahead, n, b) for n, b in zip(now, before)], axis=1
        ).astype(jnp.bfloat16)
        before = now
        n = min(tiles, chunks - c)
        left_side = xa[c : c + n].reshape(n * 2 * rows, 2 * TILE)
        product = lax.dot_general(
            left_side, panel, (((1,), (1,)), ((), ())), preferred_element_type=jnp.float32
        )
        for i in range(n):
            part = product[i * 2 * rows : (i + 1) * 2 * rows]
            sums[i] = part if sums[i] is None else sums[i] + part

    powers = []
    for i in range(tiles):
        rounded = sums[i].astype(jnp.bfloat16).astype(jnp.float32)
        real, imag = rounded[:rows], rounded[rows:]
        power = real * real + imag * imag
        if i == 0:
            power = jnp.where(ri >= 1, power, 0.0)
        powers.append(power)
        if 1 <= i <= across:
            xf[i - 1, pl.ds(0, rows, stride=2), :] = real
            xf[i - 1, pl.ds(1, rows, stride=2), :] = imag
    for b in range(beams):
        for p in range(pulses):
            at = 2 * (b * pulses + p)
            for i in range(across):
                comp[b, p, :, i * TILE : (i + 1) * TILE] = xf[i, at : at + 2, :].astype(
                    jnp.bfloat16
                )

    split = []
    for power in powers:
        high = power.astype(jnp.bfloat16)
        rest = power - high.astype(jnp.float32)
        middle = rest.astype(jnp.bfloat16)
        low = (rest - middle.astype(jnp.float32)).astype(jnp.bfloat16)
        split.append([v.astype(jnp.float32) for v in (high, middle, low)])
    for b in range(beams):
        mine = slice(b * pulses, (b + 1) * pulses)
        side = jnp.concatenate(
            [
                jnp.concatenate([split[i + d][k][mine] for d in range(3)], axis=1)
                for i in range(across)
                for k in range(3)
            ],
            axis=0,
        ).astype(jnp.bfloat16)
        window = lax.dot_general(
            side, weights[b], (((1,), (1,)), ((), ())), preferred_element_type=jnp.float32
        )
        for i in range(across):
            base = 3 * i * pulses
            noise = (
                window[base : base + pulses]
                + window[base + pulses : base + 2 * pulses]
                + window[base + 2 * pulses : base + 3 * pulses]
            ) / counts[b, :, i * TILE : (i + 1) * TILE]
            ratio[b, :, i * TILE : (i + 1) * TILE] = powers[i + 1][mine] / (
                factors[b] * (noise + EPSILON)
            )


def body(sizes, signal, replica, guard_cells, train_cells, scale_index, offsets):
    dims = plan(signal.shape, replica.shape, sizes)
    pieces, piece, gates, total, senders, tiles, panels, chunks, keeps = dims
    beams, pulses = signal.shape[0], signal.shape[1]
    rows = beams * pulses
    width = max(chunks * TILE + OFF_MAX, TILE + gates + sum(keeps))
    vmem = pl.BlockSpec(memory_space=pltpu.VMEM)
    placed = pl.BlockSpec(memory_space=pltpu.HBM)
    reach = len(keeps)
    planes = senders // sizes[1]
    operands = (offsets, guard_cells, train_cells, scale_index, signal, replica)
    gathered = pl.pallas_call(
        functools.partial(gather, sizes, dims),
        out_shape=(
            jax.ShapeDtypeStruct((senders, 2, piece), jnp.bfloat16),
            jax.ShapeDtypeStruct((chunks, 2 * rows, 2 * TILE), jnp.bfloat16),
            jax.ShapeDtypeStruct((beams, TILE, 3 * TILE), jnp.bfloat16),
            jax.ShapeDtypeStruct((beams, pulses, gates), jnp.float32),
            jax.ShapeDtypeStruct((beams, pulses, TILE), jnp.float32),
        ),
        in_specs=[placed] * 6,
        out_specs=(vmem,) * 5,
        scratch_shapes=[
            pltpu.VMEM((senders, 2, piece), jnp.bfloat16),
            pltpu.VMEM(signal.shape, jnp.bfloat16),
            pltpu.VMEM((beams, pulses, 2, TILE), jnp.bfloat16),
            pltpu.VMEM((width // TILE, 2 * rows, TILE), jnp.float32),
            pltpu.VMEM((2 * rows, width), jnp.float32),
        ]
        + [pltpu.SMEM((beams,), jnp.int32)] * 4
        + [
            pltpu.SemaphoreType.DMA((6,)),
            pltpu.SemaphoreType.DMA((1 + 2 * planes + sizes[0], sizes[1])),
            pltpu.SemaphoreType.DMA((senders,)),
            pltpu.SemaphoreType.DMA((reach + 1,)),
            pltpu.SemaphoreType.DMA((reach + 1,)),
            pltpu.SemaphoreType.REGULAR((sizes[0] - planes + 1,)),
        ]
        + [pltpu.VMEM((beams, pulses, 2, keep), jnp.bfloat16) for keep in keeps],
        compiler_params=pltpu.CompilerParams(
            collective_id=0, has_side_effects=True, vmem_limit_bytes=GRANT
        ),
        name="gather",
    )(*[pltpu.with_memory_space_constraint(v, pltpu.HBM) for v in operands])
    return pl.pallas_call(
        functools.partial(compute, sizes, dims),
        out_shape=(
            jax.ShapeDtypeStruct(signal.shape, jnp.bfloat16),
            jax.ShapeDtypeStruct((beams, pulses, gates), jnp.float32),
        ),
        in_specs=[vmem] * 5,
        out_specs=(vmem, vmem),
        scratch_shapes=[pltpu.VMEM((gates // TILE, 2 * rows, TILE), jnp.float32)],
        compiler_params=pltpu.CompilerParams(vmem_limit_bytes=GRANT),
        name="compute",
    )(*gathered)


def solution(mesh):
    placed = (
        P("beam", "pulse", None, "range"),
        P(None, ("beam", "pulse")),
        P("beam"),
        P("beam"),
        P("beam"),
        P("beam"),
    )
    sizes = (mesh.shape["beam"], mesh.shape["pulse"], mesh.shape["range"])
    return jax.shard_map(
        functools.partial(body, sizes),
        mesh=mesh,
        in_specs=placed,
        out_specs=(P("beam", "pulse", None, "range"), P("beam", "pulse", "range")),
        check_vma=False,
    )
```
